768 devices in a mesh: seq: 12 (over z_lo, x), exp: 64 (over z_hi, y, core).
Axes of the slice: x: 4, y: 8, z: 12 (z_hi: 4, z_lo: 3; z = z_hi * 3 + z_lo), core: 2. Of those that a mesh axis runs over, the one named last changes fastest.
Arguments:
- query: bfloat16 [1536, 8192], P('seq', 'exp'), may hold values from -6 to 6
- key_in: bfloat16 [1536, 8192], P('seq', 'exp'), may hold values from -6 to 6
- value: bfloat16 [1536, 8192], P('seq', 'exp'), may hold values from -6 to 6
- decay_log: float32 [1536, 64], P('seq', 'exp'), may hold values from -1 to 0
- norm_gain: bfloat16 [8192], P('exp'), may hold values from 0.099609375 to 1.8984375
- w_out: bfloat16 [8192, 4096], P('exp'), may hold values from -0.0625 to 0.0625
- router: bfloat16 [4096, 4], replicated, may hold values from -0.09375 to 0.09375
- routes: int32 [1536, 2], P('seq'), may hold values from 0 to 3, all different within a row; in each aligned block of 128 rows (0 to 127, 128 to 255, ...) at most 96 rows name the same one
- w_gate: bfloat16 [64, 4096, 288], P('exp'), may hold values from -0.09375 to 0.09375
- w_up: bfloat16 [64, 4096, 288], P('exp'), may hold values from -0.09375 to 0.09375
- w_down: bfloat16 [64, 288, 4096], P('exp'), may hold values from -0.09375 to 0.09375
Outputs:
- output: bfloat16 [1536, 4096], P(('seq', 'exp'))
The draws below stay inside these ranges and needn't reach their ends.
Inputs may be any that keep to these rules, and one draw needn't show every extreme that they name: `routes`: among the positions of one block of 128 positions no expert is named more than 96 times, a bound that some block reaches; a position names 2 different experts.
All inputs are finite; a program needn't handle non-finite values.
Results may differ from the reference program's by a relative error of at most 0.015.
Values may be sent and summed in bfloat16 or wider, within the bound.
A program may use at most 32 MiB of HBM per device.

```python
import math
import jax
import jax.numpy as jnp
import numpy as np
from jax import lax

HEAD = 128
DM = 4096
FFW = 288
EXPERTS = 4
TOP = 2
TOK_DEV = 128
HEAD_TOTAL = 64
ATT = 8192
SLICES = 16
SLICED = 64
CAP = 96
SEQUENCE_LENGTH = 1536
N_SEQ = 12


def draw_decay_log(key, part):
    random_subkeys = jax.random.split(key, 7)
    fast_share = 0.5
    fast_heads = jax.random.bernoulli(random_subkeys[0], fast_share, (HEAD_TOTAL,))
    fast_rate = jax.random.uniform(random_subkeys[1], (HEAD_TOTAL,), jnp.float32, 1.0 / 50.0, 1.0 / 30.0)
    slow_rate = jnp.exp(jax.random.uniform(random_subkeys[2], (HEAD_TOTAL,), jnp.float32, jnp.log(0.1 / SEQUENCE_LENGTH), jnp.log(1.5 / SEQUENCE_LENGTH)))
    baseline_rate = jnp.where(fast_heads, fast_rate, slow_rate)
    jitter_level = jax.random.uniform(random_subkeys[4], (SEQUENCE_LENGTH, HEAD_TOTAL), jnp.float32, 0.5, 1.5)
    spike_mask = jax.random.bernoulli(random_subkeys[5], 3.0 / SEQUENCE_LENGTH, (SEQUENCE_LENGTH, HEAD_TOTAL))
    spike_loss = jax.random.uniform(random_subkeys[6], (SEQUENCE_LENGTH, HEAD_TOTAL), jnp.float32, 0.2, 0.5)
    return -(baseline_rate * jitter_level) + jnp.where(spike_mask, jnp.log(1.0 - spike_loss), 0.0)


def level_of(own_key, dims, pieces, smallest, top_value):
    loudness, own = 1.0, jax.random.fold_in(own_key, 6)
    for position, blocks in pieces:
        heights = jnp.exp(jax.random.uniform(jax.random.fold_in(own, position), (blocks,), jnp.float32, smallest / len(pieces), top_value / len(pieces)))
        loudness = loudness * jnp.repeat(heights, dims[position] // blocks).reshape([-1 if axis == position else 1 for axis in range(len(dims))])
    return loudness


def routed_block(rng, own, number, rows, number_of, top, reach, skew):
    sequence = jax.random.permutation(rng, number_of)
    packed, usual = portions_of(number_of, rows * top, reach, skew, True), portions_of(number_of, rows * top, reach, skew, False)
    places = jnp.arange(number_of)

    def named(sizes, turn):
        used = int((sizes > 0).sum())
        fixed = max(1, used // 4)
        shifted = fixed + (places - fixed + turn * (used - fixed)) % max(1, number_of - fixed)
        return jnp.zeros((number_of,), jnp.int32).at[sequence[jnp.where(places < fixed, places, shifted)]].set(jnp.asarray(sizes, jnp.int32))

    sizes = jnp.where(number % 4 == 0, named(packed, number // 4), named(usual, number - number // 4 - 1))
    mixed = jax.random.permutation(jax.random.fold_in(own, 3), number_of)
    source_of, receiver = mixed[0:number_of // 2 * 2:2], mixed[1:number_of // 2 * 2:2]
    room = jnp.minimum(sizes[source_of] - 1, reach - sizes[receiver]) // 2
    room = jnp.where((source_of == sequence[0]) | (receiver == sequence[0]) | (sizes[receiver] == 0), 0, jnp.maximum(room, 0))
    shifted = jax.random.randint(jax.random.fold_in(own, 4), (number_of // 2,), 0, 1 << 20) % (room + 1)
    sizes = sizes.at[source_of].add(-shifted).at[receiver].add(shifted)
    labels = jnp.searchsorted(jnp.cumsum(sizes), jnp.arange(rows * top), side="right").astype(jnp.int32)
    grid = labels.reshape(top, rows).T
    grid = grid[jax.random.permutation(jax.random.fold_in(own, 1), rows)]
    turn = jax.random.randint(jax.random.fold_in(own, 2), (rows, 1), 0, top)
    return jnp.take_along_axis(grid, (jnp.arange(top)[None, :] + turn) % top, axis=1)


def portions_of(number_of, total, most, skew, full):
    weights = [(1 << 20) // math.isqrt(rank ** skew) + 1 for rank in range(1, number_of + 1)]
    largest = most if full else min(most, max(-(-total // number_of), total * weights[0] // sum(weights)))
    least = 1 if total - largest >= number_of - 1 else 0
    given, rest = [largest] + [least] * (number_of - 1), total - largest - least * (number_of - 1)
    while rest > 0:
        candidates = [i for i in range(1, number_of) if given[i] < largest] or [i for i in range(1, number_of) if given[i] < most]
        pool, budget = sum([weights[i] for i in candidates]), rest
        for i in candidates:
            extra = min(most - given[i], max(1, budget * weights[i] // pool), rest)
            given[i] = given[i] + extra
            rest = rest - extra
    return np.array(given)


def bell_draw(key, extent, scale, limit, cuts=(), kind=jnp.bfloat16):
    array = jax.random.normal(key, extent, jnp.float32) * scale
    if len(cuts) > 0:
        array = level_of(key, extent, cuts, -0.22, 0.18) * array
    return jnp.clip(array, min=-limit, max=limit).astype(kind)


def setup_inputs(seed: int = 0) -> dict:
    streams_of = jax.random.split(jax.random.key(seed), 12)
    query = bell_draw(streams_of[0], (SEQUENCE_LENGTH, ATT), 1.0, 6.0, ((0, 12), (1, 64)))
    key_in = bell_draw(streams_of[1], (SEQUENCE_LENGTH, ATT), 1.0, 6.0, ((0, 12), (1, 64)))
    value = bell_draw(streams_of[2], (SEQUENCE_LENGTH, ATT), 1.0, 6.0, ((0, 12), (1, 64)))
    decay_log = draw_decay_log(jax.random.fold_in(streams_of[11], 71), 0)
    norm_gain = jnp.clip(1.0 + 0.18 * jax.random.normal(streams_of[4], (ATT,), jnp.float32), 0.099609375, 1.8984375).astype(jnp.bfloat16)
    w_out = bell_draw(streams_of[5], (ATT, DM), ATT ** -0.5, 0.0625, ((0, 64),))
    router = bell_draw(streams_of[6], (DM, EXPERTS), DM ** -0.5, 0.09375)
    routes_keys = jax.random.split(jax.random.fold_in(streams_of[7], 1), SEQUENCE_LENGTH // TOK_DEV)
    routes_turns = jax.random.permutation(jax.random.fold_in(streams_of[7], 3), SEQUENCE_LENGTH // TOK_DEV)
    routes = jax.vmap(lambda own, number: routed_block(jax.random.fold_in(streams_of[7], 2), own, number, TOK_DEV, EXPERTS, TOP, CAP, 2))(routes_keys, routes_turns).reshape((SEQUENCE_LENGTH, TOP))
    w_gate = bell_draw(streams_of[8], (SLICED, DM, FFW), DM ** -0.5, 0.09375, ((0, 64),))
    w_up = bell_draw(streams_of[9], (SLICED, DM, FFW), DM ** -0.5, 0.09375, ((0, 64),))
    w_down = bell_draw(streams_of[10], (SLICED, FFW, DM), (FFW * SLICES) ** -0.5, 0.09375, ((0, 64),))
    return {"query": query, "key_in": key_in, "value": value, "decay_log": decay_log, "norm_gain": norm_gain, "w_out": w_out, "router": router, "routes": routes, "w_gate": w_gate, "w_up": w_up, "w_down": w_down}


def attend_block(state, block):
    query_blk, key_blk, value_blk, decay_blk = block
    query_f32 = query_blk.astype(jnp.float32)
    key_f32 = key_blk.astype(jnp.float32)
    value_f32 = value_blk.astype(jnp.float32)
    cumulative = jnp.cumsum(decay_blk, axis=0)
    scores = jnp.einsum('thd,shd->hts', query_f32, key_f32)
    spread = cumulative.T[:, :, None] - cumulative.T[:, None, :]
    causal = jnp.arange(TOK_DEV, dtype=jnp.int32)[:, None] >= jnp.arange(TOK_DEV, dtype=jnp.int32)[None, :]
    weights = jnp.where(causal, jnp.exp(jnp.where(causal, spread, 0.0)), 0.0)
    attend = (scores * weights / HEAD).astype(jnp.bfloat16)
    intra_part = jnp.einsum('hts,she->the', attend.astype(jnp.float32), value_f32)
    inter_part = jnp.exp(cumulative)[:, :, None] * jnp.einsum('thd,hde->the', query_f32, state, precision=lax.Precision.HIGHEST) / HEAD
    totals = cumulative[-1]
    tail_decay = jnp.exp(totals[None, :] - cumulative)
    state_delta = jnp.einsum('shd,she->hde', key_f32 * tail_decay[:, :, None], value_f32, precision=lax.Precision.HIGHEST)
    new_state = jnp.exp(totals)[:, None, None] * state + state_delta
    return (new_state, intra_part + inter_part)

def reference(query, key_in, value, decay_log, norm_gain, w_out, router, routes, w_gate, w_up, w_down):
    blocks = (query.reshape(N_SEQ, TOK_DEV, HEAD_TOTAL, HEAD), key_in.reshape(N_SEQ, TOK_DEV, HEAD_TOTAL, HEAD), value.reshape(N_SEQ, TOK_DEV, HEAD_TOTAL, HEAD), decay_log.reshape(N_SEQ, TOK_DEV, HEAD_TOTAL))
    start_state = jnp.zeros((HEAD_TOTAL, HEAD, HEAD), jnp.float32)
    _, attended = lax.scan(attend_block, start_state, blocks)
    attended = attended.reshape(SEQUENCE_LENGTH, HEAD_TOTAL, HEAD)
    inverse_rms = lax.rsqrt(lax.optimization_barrier(jnp.mean(attended * attended, axis=-1, keepdims=True)) + 1e-06)
    gain_f32 = norm_gain.astype(jnp.float32).reshape(HEAD_TOTAL, HEAD)
    normed = (attended * inverse_rms * gain_f32).astype(jnp.bfloat16).reshape(SEQUENCE_LENGTH, ATT)
    mixed = jnp.dot(normed, w_out, preferred_element_type=jnp.float32).astype(jnp.bfloat16)
    logits = jnp.dot(mixed, router, preferred_element_type=jnp.float32)
    picked = jnp.take_along_axis(logits, routes, axis=1)
    raised = jnp.exp(picked)
    gate_probs = raised / lax.optimization_barrier(jnp.sum(raised, axis=-1, keepdims=True))
    block_ids = routes.reshape(N_SEQ, TOK_DEV * TOP)
    onehot = (block_ids[:, :, None] == jnp.arange(EXPERTS, dtype=jnp.int32)[None, None, :]).astype(jnp.int32)
    earlier_hits = jnp.cumsum(onehot, axis=1) - onehot
    slot_index = lax.optimization_barrier(jnp.sum(earlier_hits * onehot, axis=-1))
    target = (jnp.arange(N_SEQ, dtype=jnp.int32)[:, None] * CAP + slot_index).reshape(-1).astype(jnp.int32)
    flat_ids = block_ids.reshape(-1).astype(jnp.int32)
    token_ids = (jnp.arange(SEQUENCE_LENGTH * TOP, dtype=jnp.int32) // TOP).astype(jnp.int32)
    slot_table = jnp.full((EXPERTS, N_SEQ * CAP), -1, jnp.int32).at[flat_ids, target].set(token_ids)
    gate_full = w_gate.reshape(EXPERTS, SLICES, DM, FFW).transpose(0, 2, 1, 3).reshape(EXPERTS, DM, SLICES * FFW)
    up_full = w_up.reshape(EXPERTS, SLICES, DM, FFW).transpose(0, 2, 1, 3).reshape(EXPERTS, DM, SLICES * FFW)
    down_full = w_down.reshape(EXPERTS, SLICES * FFW, DM)

    def expert_run(expert_cols):
        table_row, gate_w, up_w, down_w = expert_cols
        rows = mixed[jnp.maximum(table_row, 0)]
        gate_part = jnp.dot(rows, gate_w, preferred_element_type=jnp.float32)
        up_part = jnp.dot(rows, up_w, preferred_element_type=jnp.float32)
        hidden = (jax.nn.silu(gate_part) * up_part).astype(jnp.bfloat16)
        return jnp.dot(hidden, down_w, preferred_element_type=jnp.float32)
    expert_outs = lax.map(expert_run, (slot_table, gate_full, up_full, down_full))
    row_out = expert_outs[flat_ids, target].reshape(SEQUENCE_LENGTH, TOP, DM)
    combined = lax.optimization_barrier(jnp.sum(row_out * gate_probs[:, :, None], axis=1))
    return (mixed.astype(jnp.float32) + combined).astype(jnp.bfloat16)
```

```python
import jax
import jax.numpy as jnp
from jax import lax
from jax.experimental import pallas as pl
from jax.experimental.pallas import tpu as pltpu
from jax.sharding import PartitionSpec as P

MESH = pl.DeviceIdType.MESH
F32, BF16 = jnp.float32, jnp.bfloat16

NX, NZL, NY, NZH = 4, 3, 8, 4
TOK, HEAD, DM, FFW, EXPERTS = 128, 128, 4096, 288, 4
HALF = DM // 2
CH = TOK // NY
GR = CH // NZH
FPAD = 384
NP = 4
W = HALF // NP
PACK = TOK + 16


def hops_of(piece):
    return (4, 3) if piece % 2 == 0 else (3, 4)


def cols_of(piece):
    return slice(piece * W, (piece + 1) * W)


def dot(a, b):
    return jnp.dot(a, b, preferred_element_type=F32)


def dot_nt(a, b):
    return lax.dot_general(a, b, (((1,), (1,)), ((), ())), preferred_element_type=F32)


def dot_tn(a, b):
    return lax.dot_general(a, b, (((0,), (0,)), ((), ())), preferred_element_type=F32)


def log_rows(total):
    high = total.astype(BF16)
    rest = total - high.astype(F32)
    mid = rest.astype(BF16)
    low = (rest - mid.astype(F32)).astype(BF16)
    row = lax.broadcasted_iota(jnp.int32, (16, HEAD), 0)
    return jnp.where(
        row == 0, high.astype(F32), jnp.where(row == 1, mid.astype(F32), low.astype(F32))
    ).astype(BF16)


def log_of(rows):
    rows = rows.astype(F32)
    return rows[0:1] + rows[1:2] + rows[2:3]


def kernel(
    q_hbm, k_hbm, v_hbm, dec_hbm, gain_hbm, wo_hbm, rt_hbm, routes_hbm, wg_hbm, wu_hbm, wd_hbm,
    out_ref,
    q_v, k_v, v_v, dec_v, gain_v, wo2, rt_v, routes_v, wg_v, wu_v, wd2,
    st_s, st_r, rw_s, rw_r, s_in, nb, part, s1, r1, acc_v, z_s, z_r, mx, hb, s2, r2,
    zh_acc, zh_s, zh_r, fin_s, fin_r,
    ld, st_ss, st_rs, rw_ss, rw_rs, pr_ss, pr_rs, s1_ss, s1_rs, z_ss, z_rs, ag_ss, ag_rs, pf_ss, pf_rs,
    s2_ss, s2_rs, zh_ss, zh_rs,
):
    seq = lax.axis_index("seq")
    ex = lax.axis_index("exp")
    zl, x = seq // NX, seq % NX
    c = ex % 2
    y = (ex // 2) % NY
    zh = ex // (2 * NY)

    def exp_id(zh_, y_, c_):
        return (zh_ * NY + y_) * 2 + c_

    partner = (seq, exp_id(zh, y, 1 - c))
    up = (seq, exp_id(zh, (y + 1) % NY, c))
    down = (seq, exp_id(zh, (y + NY - 1) % NY, c))
    ynb = (up, down)
    za_i, zb_i = zh + 1 - 2 * (zh % 2), NZH - 1 - zh
    za, zb = (seq, exp_id(za_i, y, c)), (seq, exp_id(zb_i, y, c))
    row_peers = [(zl * NX + (x + d) % NX, ex) for d in (1, 2, 3)]
    col_peers = [(((zl + d) % NZL) * NX + x, ex) for d in (1, 2)]

    barrier = pltpu.get_barrier_semaphore()
    peers = [partner, up, down, za, zb] + row_peers + col_peers
    for peer in peers:
        pl.semaphore_signal(barrier, inc=1, device_id=peer, device_id_type=MESH)

    half = pl.multiple_of(c * HALF, HALF)
    other = pl.multiple_of((1 - c) * HALF, HALF)
    loads = [
        pltpu.make_async_copy(src, dst, ld.at[i])
        for i, (src, dst) in enumerate(
            [
                (k_hbm, k_v),
                (v_hbm, v_v),
                (dec_hbm, dec_v),
                (q_hbm, q_v),
                (gain_hbm, gain_v),
                (routes_hbm, routes_v),
                (wo_hbm.at[:, pl.ds(half, HALF)], wo2.at[0:HEAD]),
                (rt_hbm, rt_v),
                (wg_hbm, wg_v),
                (wu_hbm, wu_v),
                (wd_hbm.at[:, pl.ds(half, HALF)], wd2.at[0:FFW]),
            ]
        )
    ]
    for load in loads:
        load.start()

    def remote(src, dst, send, recv, device):
        return pltpu.make_async_remote_copy(
            src_ref=src, dst_ref=dst, send_sem=send, recv_sem=recv,
            device_id=device, device_id_type=MESH,
        )

    sent = []

    def push(*args):
        copy = remote(*args)
        copy.start()
        sent.append(copy)
        return copy

    row_i = lax.broadcasted_iota(jnp.int32, (TOK, TOK), 0)
    col_i = lax.broadcasted_iota(jnp.int32, (TOK, TOK), 1)
    tok_i = (row_i % CH) // GR * (NY * GR) + row_i // CH * GR + row_i % GR

    loads[2].wait()
    dec_row = dec_v[...]
    dec_full = jnp.broadcast_to(dec_row, (TOK, TOK))
    dec_col = jnp.sum(jnp.where(row_i == col_i, dec_full, 0.0), axis=1, keepdims=True)
    cum_row = jnp.sum(jnp.where(row_i <= col_i, dec_col, 0.0), axis=0, keepdims=True)
    cum_col = jnp.sum(jnp.where(col_i <= row_i, dec_full, 0.0), axis=1, keepdims=True)
    cum_tok = jnp.sum(jnp.where(col_i <= tok_i, dec_full, 0.0), axis=1, keepdims=True)
    total = jnp.broadcast_to(jnp.sum(dec_row, axis=1, keepdims=True), (1, HEAD))
    loads[0].wait()
    loads[1].wait()
    tail = jnp.exp(total[:, 0:1] - cum_col)
    keys = k_v[...]
    values = v_v[...]
    delta = dot_tn((keys.astype(F32) * tail).astype(BF16), values)
    st_s[0:TOK, :] = delta.astype(BF16)
    st_s[TOK:PACK, :] = log_rows(total)

    pl.semaphore_wait(barrier, len(peers))
    for d in (1, 2, 3):
        push(st_s, st_r.at[d - 1], st_ss.at[d - 1], st_rs.at[d - 1], row_peers[d - 1])
    wo_copy = push(
        wo_hbm.at[:, pl.ds(other, HALF)], wo2.at[HEAD : 2 * HEAD], pr_ss.at[0], pr_rs.at[0], partner
    )
    wd_copy = push(
        wd_hbm.at[:, pl.ds(other, HALF)], wd2.at[FPAD : FPAD + FFW], pr_ss.at[1], pr_rs.at[1], partner
    )
    wd2[FFW:FPAD, :] = jnp.zeros((FPAD - FFW, HALF), BF16)
    wd2[FPAD + FFW : 2 * FPAD, :] = jnp.zeros((FPAD - FFW, HALF), BF16)

    loads[3].wait()
    to_rows = jnp.where(col_i == tok_i, 1.0, 0.0).astype(BF16)
    queries = dot(to_rows, q_v[...]).astype(BF16)
    causal = col_i <= tok_i
    scores = dot_nt(queries, keys)
    weights = jnp.where(causal, jnp.exp(jnp.where(causal, cum_tok - cum_row, 0.0)), 0.0)
    intra = dot((scores * weights / HEAD).astype(BF16), values)

    loads[5].wait()
    routes = routes_v[...].astype(F32)
    wanted = [
        jnp.sum(
            jnp.where(col_i == tok_i, jnp.broadcast_to(routes[k : k + 1], (TOK, TOK)), 0.0),
            axis=1,
            keepdims=True,
        )
        for k in (0, 1)
    ]

    for d in (1, 2, 3):
        remote(
            st_s, st_r.at[d - 1], st_ss.at[d - 1], st_rs.at[d - 1], row_peers[d - 1]
        ).wait_recv()
    logs = [log_of(st_r[d - 1, TOK:PACK, :]) for d in (1, 2, 3)]
    states = [st_r[d - 1, 0:TOK, :].astype(F32) for d in (1, 2, 3)]
    zero = jnp.zeros_like(total)
    before = [(d <= x) for d in (1, 2, 3)]
    after_sum = sum((jnp.where(before[d], zero, logs[d]) for d in range(3)), zero)
    before_sum = sum((jnp.where(before[d], logs[d], zero) for d in range(3)), zero)
    prefix = jnp.zeros((TOK, HEAD), F32)
    row_total = jnp.exp(after_sum) * delta
    near, far = zero, zero
    for d in range(3):
        prefix = prefix + jnp.where(before[d], jnp.exp(near), zero) * states[d]
        reach = jnp.where(before[d], near + total + after_sum, far)
        row_total = row_total + jnp.exp(reach) * states[d]
        near = near + logs[d]
        far = far + jnp.where(before[d], zero, logs[d])
    rw_s[0:TOK, :] = row_total.astype(BF16)
    rw_s[TOK:PACK, :] = log_rows(total + before_sum + after_sum)
    s_in[...] = prefix

    rows_up = [
        remote(rw_s, rw_r.at[d - 1], rw_ss.at[d - 1], rw_rs.at[d - 1], col_peers[d - 1])
        for d in (1, 2)
    ]

    @pl.when(zl <= 1)
    def _():
        rows_up[0].start()

    @pl.when(zl == 0)
    def _():
        rows_up[1].start()

    @pl.when(zl >= 1)
    def _():
        rows_up[0].wait_recv()
        s_in[...] += jnp.exp(before_sum) * rw_r[0, 0:TOK, :].astype(F32)

    @pl.when(zl == 2)
    def _():
        rows_up[1].wait_recv()
        reach = before_sum + log_of(rw_r[0, TOK:PACK, :])
        s_in[...] += jnp.exp(reach) * rw_r[1, 0:TOK, :].astype(F32)

    state = s_in[...]
    state_high = state.astype(BF16)
    state_low = (state - state_high.astype(F32)).astype(BF16)
    inter = jnp.exp(cum_tok) * (dot(queries, state_high) + dot(queries, state_low)) / HEAD
    attended = intra + inter
    inverse_rms = lax.rsqrt(jnp.mean(attended * attended, axis=1, keepdims=True) + 1e-06)
    loads[4].wait()
    nb[:, 0:HEAD] = (attended * inverse_rms * gain_v[...].astype(F32)).astype(BF16)
    nb_copy = push(
        nb.at[:, 0:HEAD], nb.at[:, HEAD : 2 * HEAD], pr_ss.at[2], pr_rs.at[2], partner
    )
    loads[6].wait()
    wo_copy.wait_recv()
    nb_copy.wait_recv()

    def hop(piece, direction, left, send, recv, ssem, rsem):
        cols = cols_of(piece)
        return remote(
            send.at[direction, left - 1, :, cols],
            recv.at[direction, left - 1, :, cols],
            ssem.at[direction, left - 1, piece],
            rsem.at[direction, left - 1, piece],
            ynb[direction],
        )

    def reduce_rows(first, send, recv, ssem, rsem):
        def step(piece, direction, left, start):
            cols = cols_of(piece)
            target = (y + left) % NY if direction == 0 else (y + NY - left) % NY
            value = part[pl.ds(pl.multiple_of(target * CH, CH), CH), cols]
            if not start:
                hop(piece, direction, left + 1, send, recv, ssem, rsem).wait_recv()
                value = value + recv[direction, left, :, cols].astype(F32)
            send[direction, left - 1, :, cols] = value.astype(BF16)
            copy = hop(piece, direction, left, send, recv, ssem, rsem)
            copy.start()
            sent.append(copy)

        for piece in range(NP):
            part[:, cols_of(piece)] = first(piece)
            for direction in (0, 1):
                step(piece, direction, hops_of(piece)[direction], True)
        for t in (1, 2, 3):
            for piece in range(NP):
                for direction in (0, 1):
                    left = hops_of(piece)[direction] - t
                    if left >= 1:
                        step(piece, direction, left, False)
        for piece in range(NP):
            cols = cols_of(piece)
            value = part[pl.ds(pl.multiple_of(y * CH, CH), CH), cols]
            for direction in (0, 1):
                hop(piece, direction, 1, send, recv, ssem, rsem).wait_recv()
                value = value + recv[direction, 0, :, cols].astype(F32)
            yield piece, value

    heads = nb[...]

    def z_copy(piece, turn):
        first_a = (piece % 2 == 0) == (turn == 0)
        cols = cols_of(piece)
        return remote(
            z_s.at[turn, :, cols], z_r.at[turn, :, cols],
            z_ss.at[turn, piece], z_rs.at[turn, piece], za if first_a else zb,
        )

    def z_send(piece, turn, value):
        z_s[turn, :, cols_of(piece)] = value.astype(BF16)
        copy = z_copy(piece, turn)
        copy.start()
        sent.append(copy)

    for piece, value in reduce_rows(
        lambda piece: dot(heads, wo2[:, cols_of(piece)]), s1, r1, s1_ss, s1_rs
    ):
        acc_v[:, cols_of(piece)] = value
        z_send(piece, 0, value)
    for piece in range(NP):
        cols = cols_of(piece)
        z_copy(piece, 0).wait_recv()
        value = acc_v[:, cols] + z_r[0, :, cols].astype(F32)
        acc_v[:, cols] = value
        z_send(piece, 1, value)

    def place(chunk, core, piece):
        return mx.at[
            pl.ds(pl.multiple_of(chunk * CH, CH), CH),
            pl.ds(pl.multiple_of(core * HALF + piece * W, W), W),
        ]

    def ring(piece, direction, h):
        back = (y + NY - h) % NY if direction == 0 else (y + h) % NY
        return back

    def relay(piece, direction, h):
        chunk = ring(piece, direction, h - 1)
        spot = place(chunk, c, piece)
        return remote(
            spot, spot, ag_ss.at[direction, h - 1, piece], ag_rs.at[direction, h - 1, piece],
            ynb[direction],
        )

    def relayed(piece, direction, h):
        spot = place(ring(piece, direction, h), c, piece)
        return remote(
            spot, spot, ag_ss.at[direction, h - 1, piece], ag_rs.at[direction, h - 1, piece],
            ynb[direction],
        )

    def hand(piece, slot, chunk, core):
        spot = place(chunk, core, piece)
        return remote(spot, spot, pf_ss.at[slot, piece], pf_rs.at[slot, piece], partner)

    def start(copy):
        copy.start()
        sent.append(copy)

    handed = []
    for piece in range(NP):
        cols = cols_of(piece)
        z_copy(piece, 1).wait_recv()
        value = acc_v[:, cols] + z_r[1, :, cols].astype(F32)
        mx[
            pl.ds(pl.multiple_of(y * CH, CH), CH),
            pl.ds(pl.multiple_of(c * HALF + piece * W, W), W),
        ] = value.astype(BF16)
        for direction in (0, 1):
            start(relay(piece, direction, 1))
        start(hand(piece, 0, y, c))
        handed.append(hand(piece, 0, y, 1 - c))
    for h in (1, 2, 3, 4):
        for piece in range(NP):
            for direction in (0, 1):
                if h > hops_of(piece)[direction]:
                    continue
                relayed(piece, direction, h).wait_recv()
                if h < hops_of(piece)[direction]:
                    start(relay(piece, direction, h + 1))
                chunk = ring(piece, direction, h)
                slot = 1 + direction * 4 + h - 1
                start(hand(piece, slot, chunk, c))
                handed.append(hand(piece, slot, chunk, 1 - c))
    for copy in handed:
        copy.wait_recv()

    for i in (7, 8, 9, 10):
        loads[i].wait()
    mixed = mx[...]
    logits = dot_nt(mixed, rt_v[...])
    lane = lax.broadcasted_iota(jnp.int32, (TOK, EXPERTS), 1).astype(F32)
    member = (wanted[0] == lane) | (wanted[1] == lane)
    raised = jnp.where(member, jnp.exp(logits), 0.0)
    mine = jnp.sum(jnp.where(lane == zh.astype(F32), raised, 0.0), axis=1, keepdims=True)
    gate = mine / jnp.sum(raised, axis=1, keepdims=True)
    gate_part = dot_nt(mixed, wg_v[...])
    up_part = dot_nt(mixed, wu_v[...])
    hidden = gate_part / (1.0 + jnp.exp(-gate_part)) * up_part * gate
    hb[:, 0:FPAD] = jnp.zeros((TOK, FPAD), BF16)
    hb[:, 0:FFW] = hidden.astype(BF16)
    hb_copy = push(hb.at[:, 0:FPAD], hb.at[:, FPAD : 2 * FPAD], pr_ss.at[3], pr_rs.at[3], partner)
    wd_copy.wait_recv()
    hb_copy.wait_recv()
    units = hb[...]

    own_rows = lax.broadcasted_iota(jnp.int32, (CH, W), 0) // GR == zh
    for piece, value in reduce_rows(
        lambda piece: dot(units, wd2[:, cols_of(piece)]), s2, r2, s2_ss, s2_rs
    ):
        cols = cols_of(piece)
        rows = mx[
            pl.ds(pl.multiple_of(y * CH, CH), CH),
            pl.ds(pl.multiple_of(c * HALF + piece * W, W), W),
        ].astype(F32)
        value = value + jnp.where(own_rows, rows, 0.0)
        for g in range(NZH):
            group = value[g * GR : (g + 1) * GR, :]
            zh_acc[g, :, cols] = group
            zh_s[g, :, cols] = group.astype(BF16)

    zab_i = NZH - 1 - za_i
    firsts = [
        push(zh_s.at[za_i], zh_r.at[0], zh_ss.at[0], zh_rs.at[0], za),
        push(zh_s.at[zab_i], zh_r.at[1], zh_ss.at[1], zh_rs.at[1], za),
    ]
    firsts[1].wait_recv()
    fin_s[...] = (zh_acc[zb_i] + zh_r[1].astype(F32)).astype(BF16)
    second = push(fin_s, zh_r.at[2], zh_ss.at[2], zh_rs.at[2], zb)
    firsts[0].wait_recv()
    value = zh_acc[zh] + zh_r[0].astype(F32)
    second.wait_recv()
    value = (value + zh_r[2].astype(F32)).astype(BF16)
    fin_r[0] = value[0:2, :]
    fin_r[1] = value[2:4, :]
    last = push(fin_r.at[1 - c], fin_r.at[2], zh_ss.at[3], zh_rs.at[3], partner)
    out_ref[:, pl.ds(half, HALF)] = fin_r[c]
    last.wait_recv()
    out_ref[:, pl.ds(other, HALF)] = fin_r[2]

    for copy in sent:
        copy.wait_send()

    @pl.when(zl <= 1)
    def _():
        rows_up[0].wait_send()

    @pl.when(zl == 0)
    def _():
        rows_up[1].wait_send()


def layer(query, key_in, value, decay_log, norm_gain, w_out, router, routes, w_gate, w_up, w_down):
    dma = pltpu.SemaphoreType.DMA
    return pl.pallas_call(
        kernel,
        out_shape=jax.ShapeDtypeStruct((2, DM), BF16),
        in_specs=[pl.BlockSpec(memory_space=pl.ANY)] * 11,
        out_specs=pl.BlockSpec(memory_space=pltpu.VMEM),
        scratch_shapes=[
            pltpu.VMEM((TOK, HEAD), BF16),
            pltpu.VMEM((TOK, HEAD), BF16),
            pltpu.VMEM((TOK, HEAD), BF16),
            pltpu.VMEM((1, TOK), F32),
            pltpu.VMEM((1, HEAD), BF16),
            pltpu.VMEM((2 * HEAD, HALF), BF16),
            pltpu.VMEM((EXPERTS, DM), BF16),
            pltpu.VMEM((2, TOK), jnp.int32),
            pltpu.VMEM((FFW, DM), BF16),
            pltpu.VMEM((FFW, DM), BF16),
            pltpu.VMEM((2 * FPAD, HALF), BF16),
            pltpu.VMEM((PACK, HEAD), BF16),
            pltpu.VMEM((3, PACK, HEAD), BF16),
            pltpu.VMEM((PACK, HEAD), BF16),
            pltpu.VMEM((2, PACK, HEAD), BF16),
            pltpu.VMEM((TOK, HEAD), F32),
            pltpu.VMEM((TOK, 2 * HEAD), BF16),
            pltpu.VMEM((TOK, HALF), F32),
            pltpu.VMEM((2, 4, CH, HALF), BF16),
            pltpu.VMEM((2, 4, CH, HALF), BF16),
            pltpu.VMEM((CH, HALF), F32),
            pltpu.VMEM((2, CH, HALF), BF16),
            pltpu.VMEM((2, CH, HALF), BF16),
            pltpu.VMEM((TOK, DM), BF16),
            pltpu.VMEM((TOK, 2 * FPAD), BF16),
            pltpu.VMEM((2, 4, CH, HALF), BF16),
            pltpu.VMEM((2, 4, CH, HALF), BF16),
            pltpu.VMEM((NZH, GR, HALF), F32),
            pltpu.VMEM((NZH, GR, HALF), BF16),
            pltpu.VMEM((3, GR, HALF), BF16),
            pltpu.VMEM((GR, HALF), BF16),
            pltpu.VMEM((3, 2, HALF), BF16),
            dma((11,)),
            dma((3,)),
            dma((3,)),
            dma((2,)),
            dma((2,)),
            dma((4,)),
            dma((4,)),
            dma((2, 4, NP)),
            dma((2, 4, NP)),
            dma((2, NP)),
            dma((2, NP)),
            dma((2, 4, NP)),
            dma((2, 4, NP)),
            dma((9, NP)),
            dma((9, NP)),
            dma((2, 4, NP)),
            dma((2, 4, NP)),
            dma((4,)),
            dma((4,)),
        ],
        compiler_params=pltpu.CompilerParams(
            collective_id=0, has_side_effects=True, vmem_limit_bytes=56 << 20
        ),
        name="layer",
    )(
        query,
        key_in,
        value,
        decay_log.T,
        norm_gain.reshape(1, HEAD),
        w_out,
        router.T,
        routes.T,
        w_gate[0].T,
        w_up[0].T,
        w_down[0],
    )


def solution(mesh):
    placed = (
        P("seq", "exp"),
        P("seq", "exp"),
        P("seq", "exp"),
        P("seq", "exp"),
        P("exp"),
        P("exp", None),
        P(),
        P("seq", None),
        P("exp", None, None),
        P("exp", None, None),
        P("exp", None, None),
    )
    return jax.shard_map(
        layer, mesh=mesh, in_specs=placed, out_specs=P(("seq", "exp"), None), check_vma=False
    )
```

```python
import jax
import jax.numpy as jnp
from jax import lax
from jax.experimental import pallas as pl
from jax.experimental.pallas import tpu as pltpu
from jax.sharding import PartitionSpec as P

MESH = pl.DeviceIdType.MESH
F32, BF16 = jnp.float32, jnp.bfloat16

NX, NZL, NY, NZH = 4, 3, 8, 4
TOK, HEAD, DM, FFW, EXPERTS = 128, 128, 4096, 288, 4
HALF = DM // 2
CH = TOK // NY
GR = CH // NZH
FPAD = 384
NP = 2
W = HALF // NP
PACK = TOK + 16


def cols_of(piece):
    return slice(piece * W, (piece + 1) * W)


def dot(a, b):
    return jnp.dot(a, b, preferred_element_type=F32)


def dot_nt(a, b):
    return lax.dot_general(a, b, (((1,), (1,)), ((), ())), preferred_element_type=F32)


def dot_tn(a, b):
    return lax.dot_general(a, b, (((0,), (0,)), ((), ())), preferred_element_type=F32)


def log_rows(total):
    high = total.astype(BF16)
    rest = total - high.astype(F32)
    mid = rest.astype(BF16)
    low = (rest - mid.astype(F32)).astype(BF16)
    row = lax.broadcasted_iota(jnp.int32, (16, HEAD), 0)
    return jnp.where(
        row == 0, high.astype(F32), jnp.where(row == 1, mid.astype(F32), low.astype(F32))
    ).astype(BF16)


def log_of(rows):
    rows = rows.astype(F32)
    return rows[0:1] + rows[1:2] + rows[2:3]


def kernel(
    q_hbm, k_hbm, v_hbm, dec_hbm, gain_hbm, wo_hbm, rt_hbm, routes_hbm, wg_hbm, wu_hbm, wd_hbm,
    out_ref,
    q_v, k_v, v_v, dec_v, gain_v, wo2, rt_v, routes_v, wg_v, wu_v, wd2,
    st_s, st_r, rw_s, rw_r, s_in, nb, part, s1, r1, acc_v, z_s, z_r, mx, hb, s2, r2,
    f_acc, f_s, f_r, f_own,
    ld, st_ss, st_rs, rw_ss, rw_rs, pr_ss, pr_rs, s1_ss, s1_rs, z_ss, z_rs, ag_ss, ag_rs, pf_ss, pf_rs,
    s2_ss, s2_rs, f_ss, f_rs,
):
    seq = lax.axis_index("seq")
    ex = lax.axis_index("exp")
    zl, x = seq // NX, seq % NX
    c = ex % 2
    y = (ex // 2) % NY
    zh = ex // (2 * NY)

    def exp_id(zh_, y_, c_):
        return (zh_ * NY + y_) * 2 + c_

    partner = (seq, exp_id(zh, y, 1 - c))
    up = (seq, exp_id(zh, (y + 1) % NY, c))
    down = (seq, exp_id(zh, (y + NY - 1) % NY, c))
    ynb = (up, down)
    ynb2 = [(seq, exp_id(zh, (y + d) % NY, c)) for d in (2, NY - 2)]
    za_i, zb_i = zh + 1 - 2 * (zh % 2), NZH - 1 - zh
    za, zb = (seq, exp_id(za_i, y, c)), (seq, exp_id(zb_i, y, c))
    row_peers = [(zl * NX + (x + d) % NX, ex) for d in (1, 2, 3)]
    col_peers = [(((zl + d) % NZL) * NX + x, ex) for d in (1, 2)]

    barrier = pltpu.get_barrier_semaphore()
    peers = [partner, up, down, za, zb] + ynb2 + row_peers + col_peers
    for peer in peers:
        pl.semaphore_signal(barrier, inc=1, device_id=peer, device_id_type=MESH)

    half = pl.multiple_of(c * HALF, HALF)
    other = pl.multiple_of((1 - c) * HALF, HALF)
    loads = [
        pltpu.make_async_copy(src, dst, ld.at[i])
        for i, (src, dst) in enumerate(
            [
                (k_hbm, k_v),
                (v_hbm, v_v),
                (dec_hbm, dec_v),
                (q_hbm, q_v),
                (gain_hbm, gain_v),
                (routes_hbm, routes_v),
                (wo_hbm.at[:, pl.ds(half, HALF)], wo2.at[0:HEAD]),
                (rt_hbm, rt_v),
                (wg_hbm, wg_v),
                (wu_hbm, wu_v),
                (wd_hbm.at[:, pl.ds(half, HALF)], wd2.at[0:FFW]),
            ]
        )
    ]
    for load in loads:
        load.start()

    def remote(src, dst, send, recv, device):
        return pltpu.make_async_remote_copy(
            src_ref=src, dst_ref=dst, send_sem=send, recv_sem=recv,
            device_id=device, device_id_type=MESH,
        )

    sent = []

    def start(copy):
        copy.start()
        sent.append(copy)
        return copy

    def push(*args):
        return start(remote(*args))

    row_i = lax.broadcasted_iota(jnp.int32, (TOK, TOK), 0)
    col_i = lax.broadcasted_iota(jnp.int32, (TOK, TOK), 1)
    tok_i = (row_i % CH) // GR * (NY * GR) + row_i // CH * GR + row_i % GR

    loads[2].wait()
    dec_row = dec_v[...]
    dec_full = jnp.broadcast_to(dec_row, (TOK, TOK))
    dec_col = jnp.sum(jnp.where(row_i == col_i, dec_full, 0.0), axis=1, keepdims=True)
    cum_row = jnp.sum(jnp.where(row_i <= col_i, dec_col, 0.0), axis=0, keepdims=True)
    cum_col = jnp.sum(jnp.where(col_i <= row_i, dec_full, 0.0), axis=1, keepdims=True)
    cum_tok = jnp.sum(jnp.where(col_i <= tok_i, dec_full, 0.0), axis=1, keepdims=True)
    total = jnp.broadcast_to(jnp.sum(dec_row, axis=1, keepdims=True), (1, HEAD))
    loads[0].wait()
    loads[1].wait()
    tail = jnp.exp(total[:, 0:1] - cum_col)
    keys = k_v[...]
    values = v_v[...]
    delta = dot_tn((keys.astype(F32) * tail).astype(BF16), values)
    st_s[0:TOK, :] = delta.astype(BF16)
    st_s[TOK:PACK, :] = log_rows(total)

    pl.semaphore_wait(barrier, len(peers))
    for d in (1, 2, 3):
        push(st_s, st_r.at[d - 1], st_ss.at[d - 1], st_rs.at[d - 1], row_peers[d - 1])
    wo_copy = push(
        wo_hbm.at[:, pl.ds(other, HALF)], wo2.at[HEAD : 2 * HEAD], pr_ss.at[0], pr_rs.at[0], partner
    )
    wd_copy = push(
        wd_hbm.at[:, pl.ds(other, HALF)], wd2.at[FPAD : FPAD + FFW], pr_ss.at[1], pr_rs.at[1], partner
    )
    wd2[FFW:FPAD, :] = jnp.zeros((FPAD - FFW, HALF), BF16)
    wd2[FPAD + FFW : 2 * FPAD, :] = jnp.zeros((FPAD - FFW, HALF), BF16)

    loads[3].wait()
    to_rows = jnp.where(col_i == tok_i, 1.0, 0.0).astype(BF16)
    queries = dot(to_rows, q_v[...]).astype(BF16)
    causal = col_i <= tok_i
    scores = dot_nt(queries, keys)
    weights = jnp.where(causal, jnp.exp(jnp.where(causal, cum_tok - cum_row, 0.0)), 0.0)
    intra = dot((scores * weights / HEAD).astype(BF16), values)

    loads[5].wait()
    routes = routes_v[...].astype(F32)
    wanted = [
        jnp.sum(
            jnp.where(col_i == tok_i, jnp.broadcast_to(routes[k : k + 1], (TOK, TOK)), 0.0),
            axis=1,
            keepdims=True,
        )
        for k in (0, 1)
    ]

    for d in (1, 2, 3):
        remote(
            st_s, st_r.at[d - 1], st_ss.at[d - 1], st_rs.at[d - 1], row_peers[d - 1]
        ).wait_recv()
    logs = [log_of(st_r[d - 1, TOK:PACK, :]) for d in (1, 2, 3)]
    states = [st_r[d - 1, 0:TOK, :].astype(F32) for d in (1, 2, 3)]
    zero = jnp.zeros_like(total)
    before = [(d <= x) for d in (1, 2, 3)]
    after_sum = sum((jnp.where(before[d], zero, logs[d]) for d in range(3)), zero)
    before_sum = sum((jnp.where(before[d], logs[d], zero) for d in range(3)), zero)
    prefix = jnp.zeros((TOK, HEAD), F32)
    row_total = jnp.exp(after_sum) * delta
    near, far = zero, zero
    for d in range(3):
        prefix = prefix + jnp.where(before[d], jnp.exp(near), zero) * states[d]
        reach = jnp.where(before[d], near + total + after_sum, far)
        row_total = row_total + jnp.exp(reach) * states[d]
        near = near + logs[d]
        far = far + jnp.where(before[d], zero, logs[d])
    rw_s[0:TOK, :] = row_total.astype(BF16)
    rw_s[TOK:PACK, :] = log_rows(total + before_sum + after_sum)
    s_in[...] = prefix

    rows_up = [
        remote(rw_s, rw_r.at[d - 1], rw_ss.at[d - 1], rw_rs.at[d - 1], col_peers[d - 1])
        for d in (1, 2)
    ]

    @pl.when(zl <= 1)
    def _():
        rows_up[0].start()

    @pl.when(zl == 0)
    def _():
        rows_up[1].start()

    @pl.when(zl >= 1)
    def _():
        rows_up[0].wait_recv()
        s_in[...] += jnp.exp(before_sum) * rw_r[0, 0:TOK, :].astype(F32)

    @pl.when(zl == 2)
    def _():
        rows_up[1].wait_recv()
        reach = before_sum + log_of(rw_r[0, TOK:PACK, :])
        s_in[...] += jnp.exp(reach) * rw_r[1, 0:TOK, :].astype(F32)

    state = s_in[...]
    state_high = state.astype(BF16)
    state_low = (state - state_high.astype(F32)).astype(BF16)
    inter = jnp.exp(cum_tok) * (dot(queries, state_high) + dot(queries, state_low)) / HEAD
    attended = intra + inter
    inverse_rms = lax.rsqrt(jnp.mean(attended * attended, axis=1, keepdims=True) + 1e-06)
    loads[4].wait()
    nb[:, 0:HEAD] = (attended * inverse_rms * gain_v[...].astype(F32)).astype(BF16)
    nb_copy = push(
        nb.at[:, 0:HEAD], nb.at[:, HEAD : 2 * HEAD], pr_ss.at[2], pr_rs.at[2], partner
    )
    loads[6].wait()
    wo_copy.wait_recv()
    nb_copy.wait_recv()

    def span(piece, direction, role, send, recv, ssem, rsem):
        cols = cols_of(piece)
        return remote(
            send.at[direction, role, :, cols],
            recv.at[direction, role, :, cols],
            ssem.at[direction, role, piece],
            rsem.at[direction, role, piece],
            ynb[direction] if role in (0, 2) else ynb2[direction],
        )

    def chunk_at(shift, cols):
        return part[pl.ds(pl.multiple_of((y + NY + shift) % NY * CH, CH), CH), cols]

    def reduce_rows(first, send, recv, ssem, rsem):
        refs = (send, recv, ssem, rsem)
        sign = (1, -1)

        def give(piece, direction, role, value):
            send[direction, role, :, cols_of(piece)] = value.astype(BF16)
            start(span(piece, direction, role, *refs))

        for piece in range(NP):
            cols = cols_of(piece)
            part[:, cols] = first(piece)
            far = piece % 2
            give(piece, far, 1, chunk_at(4, cols))
            for d in (0, 1):
                give(piece, d, 0, chunk_at(3 * sign[d], cols))
        for piece in range(NP):
            for d in (0, 1):
                give(piece, d, 2, chunk_at(sign[d], cols_of(piece)))
        for piece in range(NP):
            cols = cols_of(piece)
            for d in (1 - piece % 2, piece % 2):
                value = chunk_at(2 * sign[d], cols)
                roles = (0, 1) if d == piece % 2 else (0,)
                for role in roles:
                    span(piece, d, role, *refs).wait_recv()
                    value = value + recv[d, role, :, cols].astype(F32)
                give(piece, d, 3, value)
        for piece in range(NP):
            cols = cols_of(piece)
            value = chunk_at(0, cols)
            for role in (2, 3):
                for d in (0, 1):
                    span(piece, d, role, *refs).wait_recv()
                    value = value + recv[d, role, :, cols].astype(F32)
            yield piece, value

    heads = nb[...]

    def z_copy(piece, turn):
        first_a = (piece % 2 == 0) == (turn == 0)
        cols = cols_of(piece)
        return remote(
            z_s.at[turn, :, cols], z_r.at[turn, :, cols],
            z_ss.at[turn, piece], z_rs.at[turn, piece], za if first_a else zb,
        )

    def z_send(piece, turn, value):
        z_s[turn, :, cols_of(piece)] = value.astype(BF16)
        start(z_copy(piece, turn))

    for piece, value in reduce_rows(
        lambda piece: dot(heads, wo2[:, cols_of(piece)]), s1, r1, s1_ss, s1_rs
    ):
        acc_v[:, cols_of(piece)] = value
        z_send(piece, 0, value)
    for piece in range(NP):
        cols = cols_of(piece)
        z_copy(piece, 0).wait_recv()
        value = acc_v[:, cols] + z_r[0, :, cols].astype(F32)
        acc_v[:, cols] = value
        z_send(piece, 1, value)

    def place(chunk, core, piece):
        return mx.at[
            pl.ds(pl.multiple_of(chunk * CH, CH), CH),
            pl.ds(pl.multiple_of(core * HALF + piece * W, W), W),
        ]

    def relay(piece, direction, far, chunk):
        spot = place(chunk, c, piece)
        to = ynb[direction] if far in (1, 3) else ynb2[direction]
        return remote(
            spot, spot, ag_ss.at[direction, far - 1, piece], ag_rs.at[direction, far - 1, piece], to
        )

    def origin(direction, far):
        return (y + NY - far) % NY if direction == 0 else (y + far) % NY

    def hand(piece, slot, chunk, core):
        spot = place(chunk, core, piece)
        return remote(spot, spot, pf_ss.at[slot, piece], pf_rs.at[slot, piece], partner)

    handed = []

    def pass_on(piece, slot, chunk):
        start(hand(piece, slot, chunk, c))
        handed.append(hand(piece, slot, chunk, 1 - c))

    for piece in range(NP):
        cols = cols_of(piece)
        z_copy(piece, 1).wait_recv()
        value = acc_v[:, cols] + z_r[1, :, cols].astype(F32)
        mx[
            pl.ds(pl.multiple_of(y * CH, CH), CH),
            pl.ds(pl.multiple_of(c * HALF + piece * W, W), W),
        ] = value.astype(BF16)
        for far in (2, 1):
            for direction in (0, 1):
                start(relay(piece, direction, far, y))
        pass_on(piece, 0, y)

    def take(piece, direction, far):
        chunk = origin(direction, far)
        relay(piece, direction, far, chunk).wait_recv()
        return chunk

    for piece in range(NP):
        for direction in (piece % 2, 1 - piece % 2):
            chunk = take(piece, direction, 2)
            if direction == piece % 2:
                start(relay(piece, direction, 4, chunk))
            start(relay(piece, direction, 3, chunk))
            pass_on(piece, 1 + direction * 4 + 1, chunk)
    for far in (1, 3, 4):
        for piece in range(NP):
            for direction in (0, 1):
                if far == 4 and direction != piece % 2:
                    continue
                chunk = take(piece, direction, far)
                pass_on(piece, 1 + direction * 4 + far - 1, chunk)

    for i in (7, 8, 9, 10):
        loads[i].wait()

    def products(columns):
        rows = mx[:, columns]
        return [dot_nt(rows, ref[:, columns]) for ref in (rt_v, wg_v, wu_v)]

    own_terms = products(pl.ds(half, HALF))
    for copy in handed:
        copy.wait_recv()
    other_terms = products(pl.ds(other, HALF))
    logits, gate_part, up_part = [a + b for a, b in zip(own_terms, other_terms)]
    lane = lax.broadcasted_iota(jnp.int32, (TOK, EXPERTS), 1).astype(F32)
    member = (wanted[0] == lane) | (wanted[1] == lane)
    raised = jnp.where(member, jnp.exp(logits), 0.0)
    mine = jnp.sum(jnp.where(lane == zh.astype(F32), raised, 0.0), axis=1, keepdims=True)
    gate = mine / jnp.sum(raised, axis=1, keepdims=True)
    hidden = gate_part / (1.0 + jnp.exp(-gate_part)) * up_part * gate
    hb[:, 0:FPAD] = jnp.zeros((TOK, FPAD), BF16)
    hb[:, 0:FFW] = hidden.astype(BF16)
    hb_copy = push(hb.at[:, 0:FPAD], hb.at[:, FPAD : 2 * FPAD], pr_ss.at[3], pr_rs.at[3], partner)
    wd_copy.wait_recv()
    hb_copy.wait_recv()
    units = hb[...]

    own_rows = lax.broadcasted_iota(jnp.int32, (CH, W), 0) // GR == zh
    for piece, value in reduce_rows(
        lambda piece: dot(units, wd2[:, cols_of(piece)]), s2, r2, s2_ss, s2_rs
    ):
        cols = cols_of(piece)
        rows = mx[
            pl.ds(pl.multiple_of(y * CH, CH), CH),
            pl.ds(pl.multiple_of(c * HALF + piece * W, W), W),
        ].astype(F32)
        value = value + jnp.where(own_rows, rows, 0.0)
        for g in range(NZH):
            for k in (0, 1):
                rows = value[g * GR + 2 * k : g * GR + 2 * k + 2, :]
                f_acc[g, k, :, cols] = rows
                f_s[g, k, :, cols] = rows.astype(BF16)

    for d in (2, 1, 3):
        to = (zh + d) % NZH
        for k in (0, 1):
            push(
                f_s.at[to, k], f_r.at[d - 1, c], f_ss.at[d - 1, k], f_rs.at[d - 1, c],
                (seq, exp_id(to, y, k)),
            )
    push(f_acc.at[zh, 1 - c], f_own.at[c], f_ss.at[3, 0], f_rs.at[3, 0], partner)
    f_own[c] = f_acc[zh, c]
    remote(f_acc.at[zh, 1 - c], f_own.at[1 - c], f_ss.at[3, 0], f_rs.at[3, 0], partner).wait_recv()
    for d in (1, 3, 2):
        for k in (0, 1):
            remote(
                f_s.at[0, k], f_r.at[d - 1, k], f_ss.at[d - 1, k], f_rs.at[d - 1, k], partner
            ).wait_recv()
    for k in (0, 1):
        value = f_own[k]
        for d in range(3):
            value = value + f_r[d, k].astype(F32)
        out_ref[:, k * HALF : (k + 1) * HALF] = value.astype(BF16)

    for copy in sent:
        copy.wait_send()

    @pl.when(zl <= 1)
    def _():
        rows_up[0].wait_send()

    @pl.when(zl == 0)
    def _():
        rows_up[1].wait_send()


def layer(query, key_in, value, decay_log, norm_gain, w_out, router, routes, w_gate, w_up, w_down):
    dma = pltpu.SemaphoreType.DMA
    return pl.pallas_call(
        kernel,
        out_shape=jax.ShapeDtypeStruct((2, DM), BF16),
        in_specs=[pl.BlockSpec(memory_space=pl.ANY)] * 11,
        out_specs=pl.BlockSpec(memory_space=pltpu.VMEM),
        scratch_shapes=[
            pltpu.VMEM((TOK, HEAD), BF16),
            pltpu.VMEM((TOK, HEAD), BF16),
            pltpu.VMEM((TOK, HEAD), BF16),
            pltpu.VMEM((1, TOK), F32),
            pltpu.VMEM((1, HEAD), BF16),
            pltpu.VMEM((2 * HEAD, HALF), BF16),
            pltpu.VMEM((EXPERTS, DM), BF16),
            pltpu.VMEM((2, TOK), jnp.int32),
            pltpu.VMEM((FFW, DM), BF16),
            pltpu.VMEM((FFW, DM), BF16),
            pltpu.VMEM((2 * FPAD, HALF), BF16),
            pltpu.VMEM((PACK, HEAD), BF16),
            pltpu.VMEM((3, PACK, HEAD), BF16),
            pltpu.VMEM((PACK, HEAD), BF16),
            pltpu.VMEM((2, PACK, HEAD), BF16),
            pltpu.VMEM((TOK, HEAD), F32),
            pltpu.VMEM((TOK, 2 * HEAD), BF16),
            pltpu.VMEM((TOK, HALF), F32),
            pltpu.VMEM((2, 4, CH, HALF), BF16),
            pltpu.VMEM((2, 4, CH, HALF), BF16),
            pltpu.VMEM((CH, HALF), F32),
            pltpu.VMEM((2, CH, HALF), BF16),
            pltpu.VMEM((2, CH, HALF), BF16),
            pltpu.VMEM((TOK, DM), BF16),
            pltpu.VMEM((TOK, 2 * FPAD), BF16),
            pltpu.VMEM((2, 4, CH, HALF), BF16),
            pltpu.VMEM((2, 4, CH, HALF), BF16),
            pltpu.VMEM((NZH, 2, 2, HALF), F32),
            pltpu.VMEM((NZH, 2, 2, HALF), BF16),
            pltpu.VMEM((3, 2, 2, HALF), BF16),
            pltpu.VMEM((2, 2, HALF), F32),
            dma((11,)),
            dma((3,)),
            dma((3,)),
            dma((2,)),
            dma((2,)),
            dma((4,)),
            dma((4,)),
            dma((2, 4, NP)),
            dma((2, 4, NP)),
            dma((2, NP)),
            dma((2, NP)),
            dma((2, 4, NP)),
            dma((2, 4, NP)),
            dma((9, NP)),
            dma((9, NP)),
            dma((2, 4, NP)),
            dma((2, 4, NP)),
            dma((4, 2)),
            dma((4, 2)),
        ],
        compiler_params=pltpu.CompilerParams(
            collective_id=0, has_side_effects=True, vmem_limit_bytes=56 << 20
        ),
        name="layer",
    )(
        query,
        key_in,
        value,
        decay_log.T,
        norm_gain.reshape(1, HEAD),
        w_out,
        router.T,
        routes.T,
        w_gate[0].T,
        w_up[0].T,
        w_down[0],
    )


def solution(mesh):
    placed = (
        P("seq", "exp"),
        P("seq", "exp"),
        P("seq", "exp"),
        P("seq", "exp"),
        P("exp"),
        P("exp", None),
        P(),
        P("seq", None),
        P("exp", None, None),
        P("exp", None, None),
        P("exp", None, None),
    )
    return jax.shard_map(
        layer, mesh=mesh, in_specs=placed, out_specs=P(("seq", "exp"), None), check_vma=False
    )
```

```python
import jax
import jax.numpy as jnp
from jax import lax
from jax.experimental import pallas as pl
from jax.experimental.pallas import tpu as pltpu
from jax.sharding import PartitionSpec as P

MESH = pl.DeviceIdType.MESH
F32, BF16 = jnp.float32, jnp.bfloat16

NX, NZL, NY, NZH = 4, 3, 8, 4
TOK, HEAD, DM, FFW, EXPERTS = 128, 128, 4096, 288, 4
HALF = DM // 2
CH = TOK // NY
GR = CH // NZH
FPAD = 384
NP = 4
W = HALF // NP
PACK = TOK + 16


def cols_of(piece):
    return slice(piece * W, (piece + 1) * W)


def dot(a, b):
    return jnp.dot(a, b, preferred_element_type=F32)


def dot_nt(a, b):
    return lax.dot_general(a, b, (((1,), (1,)), ((), ())), preferred_element_type=F32)


def dot_tn(a, b):
    return lax.dot_general(a, b, (((0,), (0,)), ((), ())), preferred_element_type=F32)


def log_rows(total):
    high = total.astype(BF16)
    rest = total - high.astype(F32)
    mid = rest.astype(BF16)
    low = (rest - mid.astype(F32)).astype(BF16)
    row = lax.broadcasted_iota(jnp.int32, (16, HEAD), 0)
    return jnp.where(
        row == 0, high.astype(F32), jnp.where(row == 1, mid.astype(F32), low.astype(F32))
    ).astype(BF16)


def log_of(rows):
    rows = rows.astype(F32)
    return rows[0:1] + rows[1:2] + rows[2:3]


def kernel(
    q_hbm, k_hbm, v_hbm, dec_hbm, gain_hbm, wo_hbm, rt_hbm, routes_hbm, wg_hbm, wu_hbm, wd_hbm,
    out_ref,
    q_v, k_v, v_v, dec_v, gain_v, wo2, rt_v, routes_v, wg_v, wu_v, wd2,
    st_s, st_r, rw_s, rw_r, s_in, nb, part, s1, r1, acc_v, z_s, z_r, mx, hb, s2, r2,
    f_acc, f_s, f_r, f_own,
    ld, st_ss, st_rs, rw_ss, rw_rs, pr_ss, pr_rs, s1_ss, s1_rs, z_ss, z_rs, ag_ss, ag_rs, pf_ss, pf_rs,
    s2_ss, s2_rs, f_ss, f_rs,
):
    seq = lax.axis_index("seq")
    ex = lax.axis_index("exp")
    zl, x = seq // NX, seq % NX
    c = ex % 2
    y = (ex // 2) % NY
    zh = ex // (2 * NY)

    def exp_id(zh_, y_, c_):
        return (zh_ * NY + y_) * 2 + c_

    partner = (seq, exp_id(zh, y, 1 - c))
    up = (seq, exp_id(zh, (y + 1) % NY, c))
    down = (seq, exp_id(zh, (y + NY - 1) % NY, c))
    ynb = (up, down)
    ynb2 = [(seq, exp_id(zh, (y + d) % NY, c)) for d in (2, NY - 2)]
    za_i, zb_i = zh + 1 - 2 * (zh % 2), NZH - 1 - zh
    za, zb = (seq, exp_id(za_i, y, c)), (seq, exp_id(zb_i, y, c))
    row_peers = [(zl * NX + (x + d) % NX, ex) for d in (1, 2, 3)]
    col_peers = [(((zl + d) % NZL) * NX + x, ex) for d in (1, 2)]

    half = pl.multiple_of(c * HALF, HALF)
    other = pl.multiple_of((1 - c) * HALF, HALF)
    loads = [
        pltpu.make_async_copy(src, dst, ld.at[i])
        for i, (src, dst) in enumerate(
            [
                (dec_hbm, dec_v),
                (k_hbm, k_v),
                (v_hbm, v_v),
                (q_hbm, q_v),
                (gain_hbm, gain_v),
                (routes_hbm, routes_v),
                (wo_hbm.at[:, pl.ds(half, HALF)], wo2.at[0:HEAD]),
                (rt_hbm, rt_v),
                (wg_hbm, wg_v),
                (wu_hbm, wu_v),
                (wd_hbm.at[:, pl.ds(half, HALF)], wd2.at[0:FFW]),
            ]
        )
    ]
    for load in loads[:3]:
        load.start()
    barrier = pltpu.get_barrier_semaphore()
    peers = [partner, up, down, za, zb] + ynb2 + row_peers + col_peers
    for peer in peers:
        pl.semaphore_signal(barrier, inc=1, device_id=peer, device_id_type=MESH)
    for load in loads[3:]:
        load.start()

    def remote(src, dst, send, recv, device):
        return pltpu.make_async_remote_copy(
            src_ref=src, dst_ref=dst, send_sem=send, recv_sem=recv,
            device_id=device, device_id_type=MESH,
        )

    sent = []

    def start(copy):
        copy.start()
        sent.append(copy)
        return copy

    def push(*args):
        return start(remote(*args))

    row_i = lax.broadcasted_iota(jnp.int32, (TOK, TOK), 0)
    col_i = lax.broadcasted_iota(jnp.int32, (TOK, TOK), 1)
    tok_i = (row_i % CH) // GR * (NY * GR) + row_i // CH * GR + row_i % GR

    loads[0].wait()
    dec_row = dec_v[...]
    dec_full = jnp.broadcast_to(dec_row, (TOK, TOK))
    tail = jnp.exp(jnp.sum(jnp.where(col_i > row_i, dec_full, 0.0), axis=1, keepdims=True))
    total = jnp.broadcast_to(jnp.sum(dec_row, axis=1, keepdims=True), (1, HEAD))
    st_s[TOK:PACK, :] = log_rows(total)
    loads[1].wait()
    loads[2].wait()
    keys = k_v[...]
    values = v_v[...]
    delta = dot_tn((keys.astype(F32) * tail).astype(BF16), values)
    st_s[0:TOK, :] = delta.astype(BF16)

    pl.semaphore_wait(barrier, len(peers))
    for d in (2, 1, 3):
        push(st_s, st_r.at[d - 1], st_ss.at[d - 1], st_rs.at[d - 1], row_peers[d - 1])
    wo_copy = push(
        wo_hbm.at[:, pl.ds(other, HALF)], wo2.at[HEAD : 2 * HEAD], pr_ss.at[0], pr_rs.at[0], partner
    )
    wd_copy = push(
        wd_hbm.at[:, pl.ds(other, HALF)], wd2.at[FPAD : FPAD + FFW], pr_ss.at[1], pr_rs.at[1], partner
    )
    wd2[FFW:FPAD, :] = jnp.zeros((FPAD - FFW, HALF), BF16)
    wd2[FPAD + FFW : 2 * FPAD, :] = jnp.zeros((FPAD - FFW, HALF), BF16)

    dec_col = jnp.sum(jnp.where(row_i == col_i, dec_full, 0.0), axis=1, keepdims=True)
    cum_row = jnp.sum(jnp.where(row_i <= col_i, dec_col, 0.0), axis=0, keepdims=True)
    cum_tok = jnp.sum(jnp.where(col_i <= tok_i, dec_full, 0.0), axis=1, keepdims=True)
    loads[3].wait()
    to_rows = jnp.where(col_i == tok_i, 1.0, 0.0).astype(BF16)
    queries = dot(to_rows, q_v[...]).astype(BF16)
    causal = col_i <= tok_i
    scores = dot_nt(queries, keys)
    weights = jnp.where(causal, jnp.exp(jnp.where(causal, cum_tok - cum_row, 0.0)), 0.0)
    intra = dot((scores * weights / HEAD).astype(BF16), values)

    loads[5].wait()
    routes = routes_v[...].astype(F32)
    wanted = [
        jnp.sum(
            jnp.where(col_i == tok_i, jnp.broadcast_to(routes[k : k + 1], (TOK, TOK)), 0.0),
            axis=1,
            keepdims=True,
        )
        for k in (0, 1)
    ]

    for d in (1, 2, 3):
        remote(
            st_s, st_r.at[d - 1], st_ss.at[d - 1], st_rs.at[d - 1], row_peers[d - 1]
        ).wait_recv()
    logs = [log_of(st_r[d - 1, TOK:PACK, :]) for d in (1, 2, 3)]
    states = [st_r[d - 1, 0:TOK, :].astype(F32) for d in (1, 2, 3)]
    zero = jnp.zeros_like(total)
    before = [(d <= x) for d in (1, 2, 3)]
    after_sum = sum((jnp.where(before[d], zero, logs[d]) for d in range(3)), zero)
    before_sum = sum((jnp.where(before[d], logs[d], zero) for d in range(3)), zero)
    prefix = jnp.zeros((TOK, HEAD), F32)
    row_total = jnp.exp(after_sum) * delta
    near, far = zero, zero
    for d in range(3):
        prefix = prefix + jnp.where(before[d], jnp.exp(near), zero) * states[d]
        reach = jnp.where(before[d], near + total + after_sum, far)
        row_total = row_total + jnp.exp(reach) * states[d]
        near = near + logs[d]
        far = far + jnp.where(before[d], zero, logs[d])
    rw_s[0:TOK, :] = row_total.astype(BF16)
    rw_s[TOK:PACK, :] = log_rows(total + before_sum + after_sum)
    s_in[...] = prefix

    rows_up = [
        remote(rw_s, rw_r.at[d - 1], rw_ss.at[d - 1], rw_rs.at[d - 1], col_peers[d - 1])
        for d in (1, 2)
    ]

    @pl.when(zl <= 1)
    def _():
        rows_up[0].start()

    @pl.when(zl == 0)
    def _():
        rows_up[1].start()

    @pl.when(zl >= 1)
    def _():
        rows_up[0].wait_recv()
        s_in[...] += jnp.exp(before_sum) * rw_r[0, 0:TOK, :].astype(F32)

    @pl.when(zl == 2)
    def _():
        rows_up[1].wait_recv()
        reach = before_sum + log_of(rw_r[0, TOK:PACK, :])
        s_in[...] += jnp.exp(reach) * rw_r[1, 0:TOK, :].astype(F32)

    state = s_in[...]
    state_high = state.astype(BF16)
    state_low = (state - state_high.astype(F32)).astype(BF16)
    inter = jnp.exp(cum_tok) * (dot(queries, state_high) + dot(queries, state_low)) / HEAD
    attended = intra + inter
    inverse_rms = lax.rsqrt(jnp.mean(attended * attended, axis=1, keepdims=True) + 1e-06)
    loads[4].wait()
    nb[:, 0:HEAD] = (attended * inverse_rms * gain_v[...].astype(F32)).astype(BF16)
    nb_copy = push(
        nb.at[:, 0:HEAD], nb.at[:, HEAD : 2 * HEAD], pr_ss.at[2], pr_rs.at[2], partner
    )
    loads[6].wait()
    wo_copy.wait_recv()
    nb_copy.wait_recv()

    def span(piece, direction, role, send, recv, ssem, rsem):
        cols = slice(0, HALF) if role == 3 else cols_of(piece)
        return remote(
            send.at[direction, role, :, cols],
            recv.at[direction, role, :, cols],
            ssem.at[direction, role, piece],
            rsem.at[direction, role, piece],
            ynb[direction] if role in (0, 3) else ynb2[direction],
        )

    def chunk_at(shift, cols):
        return part[pl.ds(pl.multiple_of((y + NY + shift) % NY * CH, CH), CH), cols]

    def reduce_rows(first, send, recv, ssem, rsem):
        refs = (send, recv, ssem, rsem)
        sign = (1, -1)

        def give(piece, direction, role, value):
            send[direction, role, :, cols_of(piece)] = value.astype(BF16)
            start(span(piece, direction, role, *refs))

        for piece in range(NP):
            cols = cols_of(piece)
            part[:, cols] = first(piece)
            far = piece % 2
            give(piece, far, 1, chunk_at(4, cols))
            for d in (0, 1):
                give(piece, d, 0, chunk_at(3 * sign[d], cols))
        for d in (0, 1):
            send[d, 3] = chunk_at(sign[d], slice(0, HALF)).astype(BF16)
            start(span(0, d, 3, *refs))
        for piece in range(NP):
            cols = cols_of(piece)
            for d in (1 - piece % 2, piece % 2):
                value = chunk_at(2 * sign[d], cols)
                roles = (0, 1) if d == piece % 2 else (0,)
                for role in roles:
                    span(piece, d, role, *refs).wait_recv()
                    value = value + recv[d, role, :, cols].astype(F32)
                give(piece, d, 2, value)
        for piece in range(NP):
            cols = cols_of(piece)
            value = chunk_at(0, cols)
            for role in (3, 2):
                for d in (0, 1):
                    if role == 2 or piece == 0:
                        span(piece, d, role, *refs).wait_recv()
                    value = value + recv[d, role, :, cols].astype(F32)
            yield piece, value

    heads = nb[...]

    def z_copy(piece, turn):
        first_a = (piece % 2 == 0) == (turn == 0)
        cols = cols_of(piece)
        return remote(
            z_s.at[turn, :, cols], z_r.at[turn, :, cols],
            z_ss.at[turn, piece], z_rs.at[turn, piece], za if first_a else zb,
        )

    def z_send(piece, turn, value):
        z_s[turn, :, cols_of(piece)] = value.astype(BF16)
        start(z_copy(piece, turn))

    for piece, value in reduce_rows(
        lambda piece: dot(heads, wo2[:, cols_of(piece)]), s1, r1, s1_ss, s1_rs
    ):
        acc_v[:, cols_of(piece)] = value
        z_send(piece, 0, value)
    for piece in range(NP):
        cols = cols_of(piece)
        z_copy(piece, 0).wait_recv()
        value = acc_v[:, cols] + z_r[0, :, cols].astype(F32)
        acc_v[:, cols] = value
        z_send(piece, 1, value)

    def place(chunk, core, piece):
        return mx.at[
            pl.ds(pl.multiple_of(chunk * CH, CH), CH),
            pl.ds(pl.multiple_of(core * HALF + piece * W, W), W),
        ]

    def whole(chunk, core):
        return mx.at[
            pl.ds(pl.multiple_of(chunk * CH, CH), CH), pl.ds(pl.multiple_of(core * HALF, HALF), HALF)
        ]

    def relay(piece, direction, far, chunk):
        spot = whole(chunk, c) if far == 1 else place(chunk, c, piece)
        to = ynb[direction] if far in (1, 3) else ynb2[direction]
        return remote(
            spot, spot, ag_ss.at[direction, far - 1, piece], ag_rs.at[direction, far - 1, piece], to
        )

    def take(piece, direction, far):
        chunk = (y + NY - far) % NY if direction == 0 else (y + far) % NY
        relay(piece, direction, far, chunk).wait_recv()
        return chunk

    def hand(slot, chunk, core):
        spot = whole(chunk, core)
        return remote(spot, spot, pf_ss.at[slot], pf_rs.at[slot], partner)

    handed = []

    def pass_on(slot, chunk):
        start(hand(slot, chunk, c))
        handed.append(hand(slot, chunk, 1 - c))

    for piece in range(NP):
        cols = cols_of(piece)
        z_copy(piece, 1).wait_recv()
        value = acc_v[:, cols] + z_r[1, :, cols].astype(F32)
        mx[
            pl.ds(pl.multiple_of(y * CH, CH), CH),
            pl.ds(pl.multiple_of(c * HALF + piece * W, W), W),
        ] = value.astype(BF16)
        for direction in (0, 1):
            start(relay(piece, direction, 2, y))
    for direction in (0, 1):
        start(relay(0, direction, 1, y))
    pass_on(0, y)
    for piece in range(NP):
        for direction in (piece % 2, 1 - piece % 2):
            chunk = take(piece, direction, 2)
            if direction == piece % 2:
                start(relay(piece, direction, 4, chunk))
            start(relay(piece, direction, 3, chunk))
            if piece == NP - 1:
                pass_on(1 + direction, chunk)
    for direction in (0, 1):
        pass_on(3 + direction, take(0, direction, 1))
    for direction in (0, 1):
        for piece in range(NP):
            chunk = take(piece, direction, 3)
        pass_on(5 + direction, chunk)
    for piece in range(NP):
        chunk = take(piece, piece % 2, 4)
    pass_on(7, chunk)

    for i in (7, 8, 9, 10):
        loads[i].wait()

    def products(columns):
        rows = mx[:, columns]
        return [dot_nt(rows, ref[:, columns]) for ref in (rt_v, wg_v, wu_v)]

    own_terms = products(pl.ds(half, HALF))
    for copy in handed:
        copy.wait_recv()
    other_terms = products(pl.ds(other, HALF))
    logits, gate_part, up_part = [a + b for a, b in zip(own_terms, other_terms)]
    lane = lax.broadcasted_iota(jnp.int32, (TOK, EXPERTS), 1).astype(F32)
    member = (wanted[0] == lane) | (wanted[1] == lane)
    raised = jnp.where(member, jnp.exp(logits), 0.0)
    mine = jnp.sum(jnp.where(lane == zh.astype(F32), raised, 0.0), axis=1, keepdims=True)
    gate = mine / jnp.sum(raised, axis=1, keepdims=True)
    hidden = gate_part / (1.0 + jnp.exp(-gate_part)) * up_part * gate
    hb[:, 0:FPAD] = jnp.zeros((TOK, FPAD), BF16)
    hb[:, 0:FFW] = hidden.astype(BF16)
    hb_copy = push(hb.at[:, 0:FPAD], hb.at[:, FPAD : 2 * FPAD], pr_ss.at[3], pr_rs.at[3], partner)
    wd_copy.wait_recv()
    hb_copy.wait_recv()
    units = hb[...]

    own_rows = lax.broadcasted_iota(jnp.int32, (CH, W), 0) // GR == zh
    for piece, value in reduce_rows(
        lambda piece: dot(units, wd2[:, cols_of(piece)]), s2, r2, s2_ss, s2_rs
    ):
        cols = cols_of(piece)
        rows = mx[
            pl.ds(pl.multiple_of(y * CH, CH), CH),
            pl.ds(pl.multiple_of(c * HALF + piece * W, W), W),
        ].astype(F32)
        value = value + jnp.where(own_rows, rows, 0.0)
        for g in range(NZH):
            for k in (0, 1):
                rows = value[g * GR + 2 * k : g * GR + 2 * k + 2, :]
                f_acc[g, k, :, cols] = rows
                f_s[g, k, :, cols] = rows.astype(BF16)

    earlier, sent[:] = list(sent), []
    for d in (2, 1, 3):
        to = (zh + d) % NZH
        for k in (0, 1):
            push(
                f_s.at[to, k], f_r.at[d - 1, c], f_ss.at[d - 1, k], f_rs.at[d - 1, c],
                (seq, exp_id(to, y, k)),
            )
    push(f_acc.at[zh, 1 - c], f_own.at[c], f_ss.at[3, 0], f_rs.at[3, 0], partner)
    f_own[c] = f_acc[zh, c]
    for copy in earlier:
        copy.wait_send()

    @pl.when(zl <= 1)
    def _():
        rows_up[0].wait_send()

    @pl.when(zl == 0)
    def _():
        rows_up[1].wait_send()

    remote(f_acc.at[zh, 1 - c], f_own.at[1 - c], f_ss.at[3, 0], f_rs.at[3, 0], partner).wait_recv()
    for d in (1, 3, 2):
        for k in (0, 1):
            remote(
                f_s.at[0, k], f_r.at[d - 1, k], f_ss.at[d - 1, k], f_rs.at[d - 1, k], partner
            ).wait_recv()
    for k in (0, 1):
        value = f_own[k]
        for d in range(3):
            value = value + f_r[d, k].astype(F32)
        out_ref[:, k * HALF : (k + 1) * HALF] = value.astype(BF16)

    for copy in sent:
        copy.wait_send()


def layer(query, key_in, value, decay_log, norm_gain, w_out, router, routes, w_gate, w_up, w_down):
    dma = pltpu.SemaphoreType.DMA
    return pl.pallas_call(
        kernel,
        out_shape=pltpu.VMEM((2, DM), BF16),
        in_specs=[pl.BlockSpec(memory_space=pl.ANY)] * 11,
        out_specs=pl.BlockSpec(memory_space=pltpu.VMEM),
        scratch_shapes=[
            pltpu.VMEM((TOK, HEAD), BF16),
            pltpu.VMEM((TOK, HEAD), BF16),
            pltpu.VMEM((TOK, HEAD), BF16),
            pltpu.VMEM((1, TOK), F32),
            pltpu.VMEM((1, HEAD), BF16),
            pltpu.VMEM((2 * HEAD, HALF), BF16),
            pltpu.VMEM((EXPERTS, DM), BF16),
            pltpu.VMEM((2, TOK), jnp.int32),
            pltpu.VMEM((FFW, DM), BF16),
            pltpu.VMEM((FFW, DM), BF16),
            pltpu.VMEM((2 * FPAD, HALF), BF16),
            pltpu.VMEM((PACK, HEAD), BF16),
            pltpu.VMEM((3, PACK, HEAD), BF16),
            pltpu.VMEM((PACK, HEAD), BF16),
            pltpu.VMEM((2, PACK, HEAD), BF16),
            pltpu.VMEM((TOK, HEAD), F32),
            pltpu.VMEM((TOK, 2 * HEAD), BF16),
            pltpu.VMEM((TOK, HALF), F32),
            pltpu.VMEM((2, 4, CH, HALF), BF16),
            pltpu.VMEM((2, 4, CH, HALF), BF16),
            pltpu.VMEM((CH, HALF), F32),
            pltpu.VMEM((2, CH, HALF), BF16),
            pltpu.VMEM((2, CH, HALF), BF16),
            pltpu.VMEM((TOK, DM), BF16),
            pltpu.VMEM((TOK, 2 * FPAD), BF16),
            pltpu.VMEM((2, 4, CH, HALF), BF16),
            pltpu.VMEM((2, 4, CH, HALF), BF16),
            pltpu.VMEM((NZH, 2, 2, HALF), F32),
            pltpu.VMEM((NZH, 2, 2, HALF), BF16),
            pltpu.VMEM((3, 2, 2, HALF), BF16),
            pltpu.VMEM((2, 2, HALF), F32),
            dma((11,)),
            dma((3,)),
            dma((3,)),
            dma((2,)),
            dma((2,)),
            dma((4,)),
            dma((4,)),
            dma((2, 4, NP)),
            dma((2, 4, NP)),
            dma((2, NP)),
            dma((2, NP)),
            dma((2, 4, NP)),
            dma((2, 4, NP)),
            dma((8,)),
            dma((8,)),
            dma((2, 4, NP)),
            dma((2, 4, NP)),
            dma((4, 2)),
            dma((4, 2)),
        ],
        compiler_params=pltpu.CompilerParams(
            collective_id=0, has_side_effects=True, vmem_limit_bytes=56 << 20
        ),
        name="layer",
    )(
        query,
        key_in,
        value,
        decay_log.T,
        norm_gain.reshape(1, HEAD),
        w_out,
        router.T,
        routes.T,
        w_gate[0].T,
        w_up[0].T,
        w_down[0],
    )


def solution(mesh):
    placed = (
        P("seq", "exp"),
        P("seq", "exp"),
        P("seq", "exp"),
        P("seq", "exp"),
        P("exp"),
        P("exp", None),
        P(),
        P("seq", None),
        P("exp", None, None),
        P("exp", None, None),
        P("exp", None, None),
    )
    return jax.shard_map(
        layer, mesh=mesh, in_specs=placed, out_specs=P(("seq", "exp"), None), check_vma=False
    )
```

```python
import jax
import jax.numpy as jnp
from jax import lax
from jax.experimental import pallas as pl
from jax.experimental.pallas import tpu as pltpu
from jax.sharding import PartitionSpec as P

MESH = pl.DeviceIdType.MESH
F32, BF16 = jnp.float32, jnp.bfloat16

NX, NZL, NY, NZH = 4, 3, 8, 4
TOK, HEAD, DM, FFW, EXPERTS = 128, 128, 4096, 288, 4
HALF = DM // 2
CH = TOK // NY
GR = CH // NZH
FPAD = 384
NP = 4
W = HALF // NP
PACK = TOK + 16


def cols_of(piece):
    return slice(piece * W, (piece + 1) * W)


def dot(a, b):
    return jnp.dot(a, b, preferred_element_type=F32)


def dot_nt(a, b):
    return lax.dot_general(a, b, (((1,), (1,)), ((), ())), preferred_element_type=F32)


def dot_tn(a, b):
    return lax.dot_general(a, b, (((0,), (0,)), ((), ())), preferred_element_type=F32)


def log_rows(total):
    high = total.astype(BF16)
    rest = total - high.astype(F32)
    mid = rest.astype(BF16)
    low = (rest - mid.astype(F32)).astype(BF16)
    row = lax.broadcasted_iota(jnp.int32, (16, HEAD), 0)
    return jnp.where(
        row == 0, high.astype(F32), jnp.where(row == 1, mid.astype(F32), low.astype(F32))
    ).astype(BF16)


def log_of(rows):
    rows = rows.astype(F32)
    return rows[0:1] + rows[1:2] + rows[2:3]


def kernel(
    q_hbm, k_hbm, v_hbm, dec_hbm, gain_hbm, wo_hbm, rt_hbm, routes_hbm, wg_hbm, wu_hbm, wd_hbm,
    out_ref,
    q_v, k_v, v_v, dec_v, gain_v, wo2, rt_v, routes_v, wg_v, wu_v, wd2,
    st_s, st_r, rw_s, rw_r, s_in, nb, part, s1, r1, acc_v, z_s, z_r, mx, hb, s2, r2,
    f_acc, f_s, f_r, f_own,
    ld, st_ss, st_rs, rw_ss, rw_rs, pr_ss, pr_rs, s1_ss, s1_rs, z_ss, z_rs, ag_ss, ag_rs, pf_ss, pf_rs,
    s2_ss, s2_rs, f_ss, f_rs,
):
    seq = lax.axis_index("seq")
    ex = lax.axis_index("exp")
    zl, x = seq // NX, seq % NX
    c = ex % 2
    y = (ex // 2) % NY
    zh = ex // (2 * NY)

    def exp_id(zh_, y_, c_):
        return (zh_ * NY + y_) * 2 + c_

    partner = (seq, exp_id(zh, y, 1 - c))
    up = (seq, exp_id(zh, (y + 1) % NY, c))
    down = (seq, exp_id(zh, (y + NY - 1) % NY, c))
    ynb = (up, down)
    ynb2 = [(seq, exp_id(zh, (y + d) % NY, c)) for d in (2, NY - 2)]
    za_i, zb_i = zh + 1 - 2 * (zh % 2), NZH - 1 - zh
    za, zb = (seq, exp_id(za_i, y, c)), (seq, exp_id(zb_i, y, c))
    row_peers = [(zl * NX + (x + d) % NX, ex) for d in (1, 2, 3)]
    col_peers = [(((zl + d) % NZL) * NX + x, ex) for d in (1, 2)]

    half = pl.multiple_of(c * HALF, HALF)
    other = pl.multiple_of((1 - c) * HALF, HALF)
    loads = [
        pltpu.make_async_copy(src, dst, ld.at[i])
        for i, (src, dst) in enumerate(
            [
                (dec_hbm, dec_v),
                (k_hbm, k_v),
                (v_hbm, v_v),
                (q_hbm, q_v),
                (gain_hbm, gain_v),
                (routes_hbm, routes_v),
                (wo_hbm.at[:, pl.ds(half, HALF)], wo2.at[0:HEAD]),
                (rt_hbm, rt_v),
                (wg_hbm, wg_v),
                (wu_hbm, wu_v),
                (wd_hbm.at[:, pl.ds(half, HALF)], wd2.at[0:FFW]),
            ]
        )
    ]
    for load in loads[:3]:
        load.start()
    barrier = pltpu.get_barrier_semaphore()
    peers = [partner, up, down, za, zb] + ynb2 + row_peers + col_peers
    for peer in peers:
        pl.semaphore_signal(barrier, inc=1, device_id=peer, device_id_type=MESH)
    for load in loads[3:]:
        load.start()

    def remote(src, dst, send, recv, device):
        return pltpu.make_async_remote_copy(
            src_ref=src, dst_ref=dst, send_sem=send, recv_sem=recv,
            device_id=device, device_id_type=MESH,
        )

    sent = []

    def start(copy):
        copy.start()
        sent.append(copy)
        return copy

    def push(*args):
        return start(remote(*args))

    row_i = lax.broadcasted_iota(jnp.int32, (TOK, TOK), 0)
    col_i = lax.broadcasted_iota(jnp.int32, (TOK, TOK), 1)
    tok_i = (row_i % CH) // GR * (NY * GR) + row_i // CH * GR + row_i % GR

    loads[0].wait()
    dec_row = dec_v[...]
    dec_full = jnp.broadcast_to(dec_row, (TOK, TOK))
    tail = jnp.exp(jnp.sum(jnp.where(col_i > row_i, dec_full, 0.0), axis=1, keepdims=True))
    total = jnp.broadcast_to(jnp.sum(dec_row, axis=1, keepdims=True), (1, HEAD))
    st_s[TOK:PACK, :] = log_rows(total)
    loads[1].wait()
    loads[2].wait()
    keys = k_v[...]
    values = v_v[...]
    delta = dot_tn((keys.astype(F32) * tail).astype(BF16), values)
    st_s[0:TOK, :] = delta.astype(BF16)

    pl.semaphore_wait(barrier, len(peers))
    for d in (2, 1, 3):
        push(st_s, st_r.at[d - 1], st_ss.at[d - 1], st_rs.at[d - 1], row_peers[d - 1])
    wo_copy = push(
        wo_hbm.at[:, pl.ds(other, HALF)], wo2.at[HEAD : 2 * HEAD], pr_ss.at[0], pr_rs.at[0], partner
    )
    wd_copy = push(
        wd_hbm.at[:, pl.ds(other, HALF)], wd2.at[FPAD : FPAD + FFW], pr_ss.at[1], pr_rs.at[1], partner
    )

    for d in (1, 2, 3):
        remote(
            st_s, st_r.at[d - 1], st_ss.at[d - 1], st_rs.at[d - 1], row_peers[d - 1]
        ).wait_recv()
    logs = [log_of(st_r[d - 1, TOK:PACK, :]) for d in (1, 2, 3)]
    states = [st_r[d - 1, 0:TOK, :].astype(F32) for d in (1, 2, 3)]
    zero = jnp.zeros_like(total)
    before = [(d <= x) for d in (1, 2, 3)]
    after_sum = sum((jnp.where(before[d], zero, logs[d]) for d in range(3)), zero)
    before_sum = sum((jnp.where(before[d], logs[d], zero) for d in range(3)), zero)
    prefix = jnp.zeros((TOK, HEAD), F32)
    row_total = jnp.exp(after_sum) * delta
    near, far = zero, zero
    for d in range(3):
        prefix = prefix + jnp.where(before[d], jnp.exp(near), zero) * states[d]
        reach = jnp.where(before[d], near + total + after_sum, far)
        row_total = row_total + jnp.exp(reach) * states[d]
        near = near + logs[d]
        far = far + jnp.where(before[d], zero, logs[d])
    rw_s[0:TOK, :] = row_total.astype(BF16)
    rw_s[TOK:PACK, :] = log_rows(total + before_sum + after_sum)
    s_in[...] = prefix

    rows_up = [
        remote(rw_s, rw_r.at[d - 1], rw_ss.at[d - 1], rw_rs.at[d - 1], col_peers[d - 1])
        for d in (1, 2)
    ]

    @pl.when(zl <= 1)
    def _():
        rows_up[0].start()

    @pl.when(zl == 0)
    def _():
        rows_up[1].start()

    dec_col = jnp.sum(jnp.where(row_i == col_i, dec_full, 0.0), axis=1, keepdims=True)
    cum_row = jnp.sum(jnp.where(row_i <= col_i, dec_col, 0.0), axis=0, keepdims=True)
    cum_tok = jnp.sum(jnp.where(col_i <= tok_i, dec_full, 0.0), axis=1, keepdims=True)
    loads[3].wait()
    to_rows = jnp.where(col_i == tok_i, 1.0, 0.0).astype(BF16)
    queries = dot(to_rows, q_v[...]).astype(BF16)
    causal = col_i <= tok_i
    scores = dot_nt(queries, keys)
    weights = jnp.where(causal, jnp.exp(jnp.where(causal, cum_tok - cum_row, 0.0)), 0.0)
    intra = dot((scores * weights / HEAD).astype(BF16), values)

    @pl.when(zl >= 1)
    def _():
        rows_up[0].wait_recv()
        s_in[...] += jnp.exp(before_sum) * rw_r[0, 0:TOK, :].astype(F32)

    @pl.when(zl == 2)
    def _():
        rows_up[1].wait_recv()
        reach = before_sum + log_of(rw_r[0, TOK:PACK, :])
        s_in[...] += jnp.exp(reach) * rw_r[1, 0:TOK, :].astype(F32)

    state = s_in[...]
    state_high = state.astype(BF16)
    state_low = (state - state_high.astype(F32)).astype(BF16)
    inter = jnp.exp(cum_tok) * (dot(queries, state_high) + dot(queries, state_low)) / HEAD
    attended = intra + inter
    inverse_rms = lax.rsqrt(jnp.mean(attended * attended, axis=1, keepdims=True) + 1e-06)
    loads[4].wait()
    nb[:, 0:HEAD] = (attended * inverse_rms * gain_v[...].astype(F32)).astype(BF16)
    nb_copy = push(
        nb.at[:, 0:HEAD], nb.at[:, HEAD : 2 * HEAD], pr_ss.at[2], pr_rs.at[2], partner
    )
    loads[6].wait()
    wo_copy.wait_recv()
    nb_copy.wait_recv()

    def span(piece, direction, role, send, recv, ssem, rsem):
        cols = slice(0, HALF) if role == 3 else cols_of(piece)
        return remote(
            send.at[direction, role, :, cols],
            recv.at[direction, role, :, cols],
            ssem.at[direction, role, piece],
            rsem.at[direction, role, piece],
            ynb[direction] if role in (0, 3) else ynb2[direction],
        )

    def chunk_at(shift, cols):
        return part[pl.ds(pl.multiple_of((y + NY + shift) % NY * CH, CH), CH), cols]

    def reduce_rows(first, send, recv, ssem, rsem):
        refs = (send, recv, ssem, rsem)
        sign = (1, -1)

        def give(piece, direction, role, value):
            send[direction, role, :, cols_of(piece)] = value.astype(BF16)
            start(span(piece, direction, role, *refs))

        for piece in range(NP):
            cols = cols_of(piece)
            part[:, cols] = first(piece)
            far = piece % 2
            give(piece, far, 1, chunk_at(4, cols))
            for d in (0, 1):
                give(piece, d, 0, chunk_at(3 * sign[d], cols))
        for d in (0, 1):
            send[d, 3] = chunk_at(sign[d], slice(0, HALF)).astype(BF16)
            start(span(0, d, 3, *refs))
        for piece in range(NP):
            cols = cols_of(piece)
            for d in (1 - piece % 2, piece % 2):
                value = chunk_at(2 * sign[d], cols)
                roles = (0, 1) if d == piece % 2 else (0,)
                for role in roles:
                    span(piece, d, role, *refs).wait_recv()
                    value = value + recv[d, role, :, cols].astype(F32)
                give(piece, d, 2, value)
        for piece in range(NP):
            cols = cols_of(piece)
            value = chunk_at(0, cols)
            for role in (3, 2):
                for d in (0, 1):
                    if role == 2 or piece == 0:
                        span(piece, d, role, *refs).wait_recv()
                    value = value + recv[d, role, :, cols].astype(F32)
            yield piece, value

    heads = nb[...]

    def z_copy(piece, turn):
        first_a = (piece % 2 == 0) == (turn == 0)
        cols = cols_of(piece)
        return remote(
            z_s.at[turn, :, cols], z_r.at[turn, :, cols],
            z_ss.at[turn, piece], z_rs.at[turn, piece], za if first_a else zb,
        )

    def z_send(piece, turn, value):
        z_s[turn, :, cols_of(piece)] = value.astype(BF16)
        start(z_copy(piece, turn))

    for piece, value in reduce_rows(
        lambda piece: dot(heads, wo2[:, cols_of(piece)]), s1, r1, s1_ss, s1_rs
    ):
        acc_v[:, cols_of(piece)] = value
        z_send(piece, 0, value)
    loads[5].wait()
    wanted = dot_nt(routes_v[...].astype(BF16), to_rows)
    wd2[FFW:FPAD, :] = jnp.zeros((FPAD - FFW, HALF), BF16)
    wd2[FPAD + FFW : 2 * FPAD, :] = jnp.zeros((FPAD - FFW, HALF), BF16)

    for piece in range(NP):
        cols = cols_of(piece)
        z_copy(piece, 0).wait_recv()
        value = acc_v[:, cols] + z_r[0, :, cols].astype(F32)
        acc_v[:, cols] = value
        z_send(piece, 1, value)

    def place(chunk, core, piece):
        return mx.at[
            pl.ds(pl.multiple_of(chunk * CH, CH), CH),
            pl.ds(pl.multiple_of(core * HALF + piece * W, W), W),
        ]

    def whole(chunk, core):
        return mx.at[
            pl.ds(pl.multiple_of(chunk * CH, CH), CH), pl.ds(pl.multiple_of(core * HALF, HALF), HALF)
        ]

    def relay(piece, direction, far, chunk):
        spot = whole(chunk, c) if far == 1 else place(chunk, c, piece)
        to = ynb[direction] if far in (1, 3) else ynb2[direction]
        return remote(
            spot, spot, ag_ss.at[direction, far - 1, piece], ag_rs.at[direction, far - 1, piece], to
        )

    def take(piece, direction, far):
        chunk = (y + NY - far) % NY if direction == 0 else (y + far) % NY
        relay(piece, direction, far, chunk).wait_recv()
        return chunk

    def hand(slot, chunk, core):
        spot = whole(chunk, core)
        return remote(spot, spot, pf_ss.at[slot], pf_rs.at[slot], partner)

    handed = []

    def pass_on(slot, chunk):
        start(hand(slot, chunk, c))
        handed.append(hand(slot, chunk, 1 - c))

    for piece in range(NP):
        cols = cols_of(piece)
        z_copy(piece, 1).wait_recv()
        value = acc_v[:, cols] + z_r[1, :, cols].astype(F32)
        mx[
            pl.ds(pl.multiple_of(y * CH, CH), CH),
            pl.ds(pl.multiple_of(c * HALF + piece * W, W), W),
        ] = value.astype(BF16)
        for direction in (0, 1):
            start(relay(piece, direction, 2, y))
    for direction in (0, 1):
        start(relay(0, direction, 1, y))
    pass_on(0, y)
    for piece in range(NP):
        for direction in (piece % 2, 1 - piece % 2):
            chunk = take(piece, direction, 2)
            if direction == piece % 2:
                start(relay(piece, direction, 4, chunk))
            start(relay(piece, direction, 3, chunk))
            if piece == NP - 1:
                pass_on(1 + direction, chunk)
    for direction in (0, 1):
        pass_on(3 + direction, take(0, direction, 1))
    for direction in (0, 1):
        for piece in range(NP):
            chunk = take(piece, direction, 3)
        pass_on(5 + direction, chunk)
    for piece in range(NP):
        chunk = take(piece, piece % 2, 4)
    pass_on(7, chunk)

    for i in (7, 8, 9, 10):
        loads[i].wait()

    def products(columns):
        rows = mx[:, columns]
        return [dot_nt(ref[:, columns], rows) for ref in (rt_v, wg_v, wu_v)]

    own_terms = products(pl.ds(half, HALF))
    for copy in handed:
        copy.wait_recv()
    other_terms = products(pl.ds(other, HALF))
    logits, gate_part, up_part = [a + b for a, b in zip(own_terms, other_terms)]
    expert = lax.broadcasted_iota(jnp.int32, (EXPERTS, TOK), 0).astype(F32)
    member = (wanted[0:1] == expert) | (wanted[1:2] == expert)
    raised = jnp.where(member, jnp.exp(logits), 0.0)
    mine = jnp.sum(jnp.where(expert == zh.astype(F32), raised, 0.0), axis=0, keepdims=True)
    gate = mine / jnp.sum(raised, axis=0, keepdims=True)
    hidden = (gate_part / (1.0 + jnp.exp(-gate_part)) * up_part * gate).T
    hb[:, 0:FPAD] = jnp.zeros((TOK, FPAD), BF16)
    hb[:, 0:FFW] = hidden.astype(BF16)
    hb_copy = push(hb.at[:, 0:FPAD], hb.at[:, FPAD : 2 * FPAD], pr_ss.at[3], pr_rs.at[3], partner)
    wd_copy.wait_recv()
    hb_copy.wait_recv()
    units = hb[...]

    own_rows = lax.broadcasted_iota(jnp.int32, (CH, W), 0) // GR == zh
    for piece, value in reduce_rows(
        lambda piece: dot(units, wd2[:, cols_of(piece)]), s2, r2, s2_ss, s2_rs
    ):
        cols = cols_of(piece)
        rows = mx[
            pl.ds(pl.multiple_of(y * CH, CH), CH),
            pl.ds(pl.multiple_of(c * HALF + piece * W, W), W),
        ].astype(F32)
        value = value + jnp.where(own_rows, rows, 0.0)
        for g in range(NZH):
            for k in (0, 1):
                rows = value[g * GR + 2 * k : g * GR + 2 * k + 2, :]
                f_acc[g, k, :, cols] = rows
                f_s[g, k, :, cols] = rows.astype(BF16)

    earlier, sent[:] = list(sent), []
    for d in (2, 1, 3):
        to = (zh + d) % NZH
        for k in (0, 1):
            push(
                f_s.at[to, k], f_r.at[d - 1, c], f_ss.at[d - 1, k], f_rs.at[d - 1, c],
                (seq, exp_id(to, y, k)),
            )
    push(f_acc.at[zh, 1 - c], f_own.at[c], f_ss.at[3, 0], f_rs.at[3, 0], partner)
    f_own[c] = f_acc[zh, c]
    for copy in earlier:
        copy.wait_send()

    @pl.when(zl <= 1)
    def _():
        rows_up[0].wait_send()

    @pl.when(zl == 0)
    def _():
        rows_up[1].wait_send()

    remote(f_acc.at[zh, 1 - c], f_own.at[1 - c], f_ss.at[3, 0], f_rs.at[3, 0], partner).wait_recv()
    for d in (1, 3, 2):
        for k in (0, 1):
            remote(
                f_s.at[0, k], f_r.at[d - 1, k], f_ss.at[d - 1, k], f_rs.at[d - 1, k], partner
            ).wait_recv()
    for k in (0, 1):
        value = f_own[k]
        for d in range(3):
            value = value + f_r[d, k].astype(F32)
        out_ref[:, k * HALF : (k + 1) * HALF] = value.astype(BF16)

    for copy in sent:
        copy.wait_send()


def layer(query, key_in, value, decay_log, norm_gain, w_out, router, routes, w_gate, w_up, w_down):
    dma = pltpu.SemaphoreType.DMA
    return pl.pallas_call(
        kernel,
        out_shape=pltpu.VMEM((2, DM), BF16),
        in_specs=[pl.BlockSpec(memory_space=pl.ANY)] * 11,
        out_specs=pl.BlockSpec(memory_space=pltpu.VMEM),
        scratch_shapes=[
            pltpu.VMEM((TOK, HEAD), BF16),
            pltpu.VMEM((TOK, HEAD), BF16),
            pltpu.VMEM((TOK, HEAD), BF16),
            pltpu.VMEM((1, TOK), F32),
            pltpu.VMEM((1, HEAD), BF16),
            pltpu.VMEM((2 * HEAD, HALF), BF16),
            pltpu.VMEM((EXPERTS, DM), BF16),
            pltpu.VMEM((2, TOK), jnp.int32),
            pltpu.VMEM((FFW, DM), BF16),
            pltpu.VMEM((FFW, DM), BF16),
            pltpu.VMEM((2 * FPAD, HALF), BF16),
            pltpu.VMEM((PACK, HEAD), BF16),
            pltpu.VMEM((3, PACK, HEAD), BF16),
            pltpu.VMEM((PACK, HEAD), BF16),
            pltpu.VMEM((2, PACK, HEAD), BF16),
            pltpu.VMEM((TOK, HEAD), F32),
            pltpu.VMEM((TOK, 2 * HEAD), BF16),
            pltpu.VMEM((TOK, HALF), F32),
            pltpu.VMEM((2, 4, CH, HALF), BF16),
            pltpu.VMEM((2, 4, CH, HALF), BF16),
            pltpu.VMEM((CH, HALF), F32),
            pltpu.VMEM((2, CH, HALF), BF16),
            pltpu.VMEM((2, CH, HALF), BF16),
            pltpu.VMEM((TOK, DM), BF16),
            pltpu.VMEM((TOK, 2 * FPAD), BF16),
            pltpu.VMEM((2, 4, CH, HALF), BF16),
            pltpu.VMEM((2, 4, CH, HALF), BF16),
            pltpu.VMEM((NZH, 2, 2, HALF), F32),
            pltpu.VMEM((NZH, 2, 2, HALF), BF16),
            pltpu.VMEM((3, 2, 2, HALF), BF16),
            pltpu.VMEM((2, 2, HALF), F32),
            dma((11,)),
            dma((3,)),
            dma((3,)),
            dma((2,)),
            dma((2,)),
            dma((4,)),
            dma((4,)),
            dma((2, 4, NP)),
            dma((2, 4, NP)),
            dma((2, NP)),
            dma((2, NP)),
            dma((2, 4, NP)),
            dma((2, 4, NP)),
            dma((8,)),
            dma((8,)),
            dma((2, 4, NP)),
            dma((2, 4, NP)),
            dma((4, 2)),
            dma((4, 2)),
        ],
        compiler_params=pltpu.CompilerParams(
            collective_id=0, has_side_effects=True, vmem_limit_bytes=56 << 20
        ),
        name="layer",
    )(
        query,
        key_in,
        value,
        decay_log.T,
        norm_gain.reshape(1, HEAD),
        w_out,
        router.T,
        routes.T,
        w_gate[0].T,
        w_up[0].T,
        w_down[0],
    )


def solution(mesh):
    placed = (
        P("seq", "exp"),
        P("seq", "exp"),
        P("seq", "exp"),
        P("seq", "exp"),
        P("exp"),
        P("exp", None),
        P(),
        P("seq", None),
        P("exp", None, None),
        P("exp", None, None),
        P("exp", None, None),
    )
    return jax.shard_map(
        layer, mesh=mesh, in_specs=placed, out_specs=P(("seq", "exp"), None), check_vma=False
    )
```

```python
import jax
import jax.numpy as jnp
from jax import lax
from jax.experimental import pallas as pl
from jax.experimental.pallas import tpu as pltpu
from jax.sharding import PartitionSpec as P

MESH = pl.DeviceIdType.MESH
F32, BF16 = jnp.float32, jnp.bfloat16

NX, NZL, NY, NZH = 4, 3, 8, 4
TOK, HEAD, DM, FFW, EXPERTS = 128, 128, 4096, 288, 4
HALF = DM // 2
CH = TOK // NY
GR = CH // NZH
FPAD = 384
NP = 4
W = HALF // NP
PACK = TOK + 16


def cols_of(piece):
    return slice(piece * W, (piece + 1) * W)


def dot(a, b):
    return jnp.dot(a, b, preferred_element_type=F32)


def dot_nt(a, b):
    return lax.dot_general(a, b, (((1,), (1,)), ((), ())), preferred_element_type=F32)


def dot_tn(a, b):
    return lax.dot_general(a, b, (((0,), (0,)), ((), ())), preferred_element_type=F32)


def log_rows(total):
    high = total.astype(BF16)
    rest = total - high.astype(F32)
    mid = rest.astype(BF16)
    low = (rest - mid.astype(F32)).astype(BF16)
    row = lax.broadcasted_iota(jnp.int32, (16, HEAD), 0)
    return jnp.where(
        row == 0, high.astype(F32), jnp.where(row == 1, mid.astype(F32), low.astype(F32))
    ).astype(BF16)


def log_of(rows):
    rows = rows.astype(F32)
    return rows[0:1] + rows[1:2] + rows[2:3]


def kernel(
    q_hbm, k_hbm, v_hbm, dec_hbm, gain_hbm, wo_hbm, rt_hbm, routes_hbm, wg_hbm, wu_hbm, wd_hbm,
    out_ref,
    q_v, k_v, v_v, dec_v, gain_v, wo2, rt_v, routes_v, wg_v, wu_v, wd2,
    st_s, st_r, rw_s, rw_r, s_in, nb, part, s1, r1, acc_v, z_s, z_r, mx, hb, s2, r2,
    f_acc, f_s, f_r, f_own,
    ld, st_ss, st_rs, rw_ss, rw_rs, pr_ss, pr_rs, s1_ss, s1_rs, z_ss, z_rs, ag_ss, ag_rs, pf_ss, pf_rs,
    s2_ss, s2_rs, f_ss, f_rs,
):
    seq = lax.axis_index("seq")
    ex = lax.axis_index("exp")
    zl, x = seq // NX, seq % NX
    c = ex % 2
    y = (ex // 2) % NY
    zh = ex // (2 * NY)

    def exp_id(zh_, y_, c_):
        return (zh_ * NY + y_) * 2 + c_

    partner = (seq, exp_id(zh, y, 1 - c))
    up = (seq, exp_id(zh, (y + 1) % NY, c))
    down = (seq, exp_id(zh, (y + NY - 1) % NY, c))
    ynb = (up, down)
    ynb2 = [(seq, exp_id(zh, (y + d) % NY, c)) for d in (2, NY - 2)]
    za_i, zb_i = zh + 1 - 2 * (zh % 2), NZH - 1 - zh
    za, zb = (seq, exp_id(za_i, y, c)), (seq, exp_id(zb_i, y, c))
    row_peers = [(zl * NX + (x + d) % NX, ex) for d in (1, 2, 3)]
    col_peers = [(((zl + d) % NZL) * NX + x, ex) for d in (1, 2)]

    half = pl.multiple_of(c * HALF, HALF)
    other = pl.multiple_of((1 - c) * HALF, HALF)
    loads = [
        pltpu.make_async_copy(src, dst, ld.at[i])
        for i, (src, dst) in enumerate(
            [
                (dec_hbm, dec_v),
                (k_hbm, k_v),
                (v_hbm, v_v),
                (q_hbm, q_v),
                (gain_hbm, gain_v),
                (routes_hbm, routes_v),
                (wo_hbm.at[:, pl.ds(half, HALF)], wo2.at[0:HEAD]),
                (rt_hbm, rt_v),
                (wg_hbm, wg_v),
                (wu_hbm, wu_v),
                (wd_hbm.at[:, pl.ds(half, HALF)], wd2.at[0:FFW]),
            ]
        )
    ]
    for load in loads[:3]:
        load.start()
    barrier = pltpu.get_barrier_semaphore()
    peers = [partner, up, down, za, zb] + ynb2 + row_peers + col_peers
    for peer in peers:
        pl.semaphore_signal(barrier, inc=1, device_id=peer, device_id_type=MESH)
    for load in loads[3:]:
        load.start()

    def remote(src, dst, send, recv, device):
        return pltpu.make_async_remote_copy(
            src_ref=src, dst_ref=dst, send_sem=send, recv_sem=recv,
            device_id=device, device_id_type=MESH,
        )

    sent = []

    def start(copy):
        copy.start()
        sent.append(copy)
        return copy

    def push(*args):
        return start(remote(*args))

    row_i = lax.broadcasted_iota(jnp.int32, (TOK, TOK), 0)
    col_i = lax.broadcasted_iota(jnp.int32, (TOK, TOK), 1)
    tok_i = (row_i % CH) // GR * (NY * GR) + row_i // CH * GR + row_i % GR

    loads[0].wait()
    dec_row = dec_v[...]
    dec_full = jnp.broadcast_to(dec_row, (TOK, TOK))
    tail = jnp.exp(jnp.sum(jnp.where(col_i > row_i, dec_full, 0.0), axis=1, keepdims=True))
    total = jnp.broadcast_to(jnp.sum(dec_row, axis=1, keepdims=True), (1, HEAD))
    st_s[TOK:PACK, :] = log_rows(total)
    loads[1].wait()
    loads[2].wait()
    keys = k_v[...]
    values = v_v[...]
    delta = dot_tn((keys.astype(F32) * tail).astype(BF16), values)
    st_s[0:TOK, :] = delta.astype(BF16)

    pl.semaphore_wait(barrier, len(peers))
    for d in (2, 1, 3):
        push(st_s, st_r.at[d - 1], st_ss.at[d - 1], st_rs.at[d - 1], row_peers[d - 1])
    wo_copy = push(
        wo_hbm.at[:, pl.ds(other, HALF)], wo2.at[HEAD : 2 * HEAD], pr_ss.at[0], pr_rs.at[0], partner
    )
    wd_copy = push(
        wd_hbm.at[:, pl.ds(other, HALF)], wd2.at[FPAD : FPAD + FFW], pr_ss.at[1], pr_rs.at[1], partner
    )

    for d in (1, 2, 3):
        remote(
            st_s, st_r.at[d - 1], st_ss.at[d - 1], st_rs.at[d - 1], row_peers[d - 1]
        ).wait_recv()
    logs = [log_of(st_r[d - 1, TOK:PACK, :]) for d in (1, 2, 3)]
    states = [st_r[d - 1, 0:TOK, :].astype(F32) for d in (1, 2, 3)]
    zero = jnp.zeros_like(total)
    before = [(d <= x) for d in (1, 2, 3)]
    after_sum = sum((jnp.where(before[d], zero, logs[d]) for d in range(3)), zero)
    before_sum = sum((jnp.where(before[d], logs[d], zero) for d in range(3)), zero)
    prefix = jnp.zeros((TOK, HEAD), F32)
    row_total = jnp.exp(after_sum) * delta
    near, far = zero, zero
    for d in range(3):
        prefix = prefix + jnp.where(before[d], jnp.exp(near), zero) * states[d]
        reach = jnp.where(before[d], near + total + after_sum, far)
        row_total = row_total + jnp.exp(reach) * states[d]
        near = near + logs[d]
        far = far + jnp.where(before[d], zero, logs[d])
    rw_s[0:TOK, :] = row_total.astype(BF16)
    rw_s[TOK:PACK, :] = log_rows(total + before_sum + after_sum)
    s_in[...] = prefix

    rows_up = [
        remote(rw_s, rw_r.at[d - 1], rw_ss.at[d - 1], rw_rs.at[d - 1], col_peers[d - 1])
        for d in (1, 2)
    ]

    @pl.when(zl <= 1)
    def _():
        rows_up[0].start()

    @pl.when(zl == 0)
    def _():
        rows_up[1].start()

    dec_col = jnp.sum(jnp.where(row_i == col_i, dec_full, 0.0), axis=1, keepdims=True)
    cum_row = jnp.sum(jnp.where(row_i <= col_i, dec_col, 0.0), axis=0, keepdims=True)
    cum_tok = jnp.sum(jnp.where(col_i <= tok_i, dec_full, 0.0), axis=1, keepdims=True)
    loads[3].wait()
    to_rows = jnp.where(col_i == tok_i, 1.0, 0.0).astype(BF16)
    queries = dot(to_rows, q_v[...]).astype(BF16)
    causal = col_i <= tok_i
    scores = dot_nt(queries, keys)
    weights = jnp.where(causal, jnp.exp(jnp.where(causal, cum_tok - cum_row, 0.0)), 0.0)
    intra = dot((scores * weights / HEAD).astype(BF16), values)

    @pl.when(zl >= 1)
    def _():
        rows_up[0].wait_recv()
        s_in[...] += jnp.exp(before_sum) * rw_r[0, 0:TOK, :].astype(F32)

    @pl.when(zl == 2)
    def _():
        rows_up[1].wait_recv()
        reach = before_sum + log_of(rw_r[0, TOK:PACK, :])
        s_in[...] += jnp.exp(reach) * rw_r[1, 0:TOK, :].astype(F32)

    state = s_in[...]
    state_high = state.astype(BF16)
    state_low = (state - state_high.astype(F32)).astype(BF16)
    inter = jnp.exp(cum_tok) * (dot(queries, state_high) + dot(queries, state_low)) / HEAD
    attended = intra + inter
    inverse_rms = lax.rsqrt(jnp.mean(attended * attended, axis=1, keepdims=True) + 1e-06)
    loads[4].wait()
    nb[:, 0:HEAD] = (attended * inverse_rms * gain_v[...].astype(F32)).astype(BF16)
    nb_copy = push(
        nb.at[:, 0:HEAD], nb.at[:, HEAD : 2 * HEAD], pr_ss.at[2], pr_rs.at[2], partner
    )
    loads[6].wait()
    wo_copy.wait_recv()
    nb_copy.wait_recv()

    def span(piece, direction, role, send, recv, ssem, rsem):
        cols = slice(0, HALF) if role == 3 else cols_of(piece)
        return remote(
            send.at[direction, role, :, cols],
            recv.at[direction, role, :, cols],
            ssem.at[direction, role, piece],
            rsem.at[direction, role, piece],
            ynb[direction] if role in (0, 3) else ynb2[direction],
        )

    def chunk_at(shift, cols):
        return part[pl.ds(pl.multiple_of((y + NY + shift) % NY * CH, CH), CH), cols]

    def reduce_rows(first, send, recv, ssem, rsem):
        refs = (send, recv, ssem, rsem)
        sign = (1, -1)

        def give(piece, direction, role, value):
            send[direction, role, :, cols_of(piece)] = value.astype(BF16)
            start(span(piece, direction, role, *refs))

        for piece in range(NP):
            cols = cols_of(piece)
            part[:, cols] = first(piece)
            far = piece % 2
            give(piece, far, 1, chunk_at(4, cols))
            for d in (0, 1):
                give(piece, d, 0, chunk_at(3 * sign[d], cols))
        for d in (0, 1):
            send[d, 3] = chunk_at(sign[d], slice(0, HALF)).astype(BF16)
            start(span(0, d, 3, *refs))
        for piece in range(NP):
            cols = cols_of(piece)
            for d in (1 - piece % 2, piece % 2):
                value = chunk_at(2 * sign[d], cols)
                roles = (0, 1) if d == piece % 2 else (0,)
                for role in roles:
                    span(piece, d, role, *refs).wait_recv()
                    value = value + recv[d, role, :, cols].astype(F32)
                give(piece, d, 2, value)
        for piece in range(NP):
            cols = cols_of(piece)
            value = chunk_at(0, cols)
            for role in (3, 2):
                for d in (0, 1):
                    if role == 2 or piece == 0:
                        span(piece, d, role, *refs).wait_recv()
                    value = value + recv[d, role, :, cols].astype(F32)
            yield piece, value

    heads = nb[...]

    def z_copy(piece, turn):
        first_a = (piece % 2 == 0) == (turn == 0)
        cols = cols_of(piece)
        return remote(
            z_s.at[turn, :, cols], z_r.at[turn, :, cols],
            z_ss.at[turn, piece], z_rs.at[turn, piece], za if first_a else zb,
        )

    def z_send(piece, turn, value):
        z_s[turn, :, cols_of(piece)] = value.astype(BF16)
        start(z_copy(piece, turn))

    for piece, value in reduce_rows(
        lambda piece: dot(heads, wo2[:, cols_of(piece)]), s1, r1, s1_ss, s1_rs
    ):
        acc_v[:, cols_of(piece)] = value
        z_send(piece, 0, value)
    loads[5].wait()
    wanted = dot_nt(routes_v[...].astype(BF16), to_rows)
    hb[:, 0:FPAD] = jnp.zeros((TOK, FPAD), BF16)
    wd2[FFW:FPAD, :] = jnp.zeros((FPAD - FFW, HALF), BF16)
    wd2[FPAD + FFW : 2 * FPAD, :] = jnp.zeros((FPAD - FFW, HALF), BF16)

    for piece in range(NP):
        cols = cols_of(piece)
        z_copy(piece, 0).wait_recv()
        value = acc_v[:, cols] + z_r[0, :, cols].astype(F32)
        acc_v[:, cols] = value
        z_send(piece, 1, value)

    def place(chunk, core, piece):
        return mx.at[
            pl.ds(pl.multiple_of(chunk * CH, CH), CH),
            pl.ds(pl.multiple_of(core * HALF + piece * W, W), W),
        ]

    def whole(chunk, core):
        return mx.at[
            pl.ds(pl.multiple_of(chunk * CH, CH), CH), pl.ds(pl.multiple_of(core * HALF, HALF), HALF)
        ]

    def relay(piece, direction, far, chunk):
        spot = whole(chunk, c) if far == 1 else place(chunk, c, piece)
        to = ynb[direction] if far in (1, 3) else ynb2[direction]
        return remote(
            spot, spot, ag_ss.at[direction, far - 1, piece], ag_rs.at[direction, far - 1, piece], to
        )

    def take(piece, direction, far):
        chunk = (y + NY - far) % NY if direction == 0 else (y + far) % NY
        relay(piece, direction, far, chunk).wait_recv()
        return chunk

    def hand(slot, chunk, core):
        spot = whole(chunk, core)
        return remote(spot, spot, pf_ss.at[slot], pf_rs.at[slot], partner)

    handed = []

    def pass_on(slot, chunk):
        start(hand(slot, chunk, c))
        handed.append(hand(slot, chunk, 1 - c))

    for piece in range(NP):
        cols = cols_of(piece)
        z_copy(piece, 1).wait_recv()
        value = acc_v[:, cols] + z_r[1, :, cols].astype(F32)
        mx[
            pl.ds(pl.multiple_of(y * CH, CH), CH),
            pl.ds(pl.multiple_of(c * HALF + piece * W, W), W),
        ] = value.astype(BF16)
        for direction in (0, 1):
            start(relay(piece, direction, 2, y))
    for direction in (0, 1):
        start(relay(0, direction, 1, y))
    pass_on(0, y)
    for piece in range(NP):
        for direction in (piece % 2, 1 - piece % 2):
            chunk = take(piece, direction, 2)
            start(relay(piece, direction, 3, chunk))
            if direction == piece % 2:
                start(relay(piece, direction, 4, chunk))
            if piece == NP - 1:
                pass_on(1 + direction, chunk)
    for direction in (0, 1):
        pass_on(3 + direction, take(0, direction, 1))
    for direction in (0, 1):
        for piece in range(NP):
            chunk = take(piece, direction, 3)
        pass_on(5 + direction, chunk)
    for piece in range(NP):
        chunk = take(piece, piece % 2, 4)
    pass_on(7, chunk)

    for i in (7, 8, 9, 10):
        loads[i].wait()

    def products(columns):
        rows = mx[:, columns]
        return [dot_nt(ref[:, columns], rows) for ref in (rt_v, wg_v, wu_v)]

    own_terms = products(pl.ds(half, HALF))
    for copy in handed:
        copy.wait_recv()
    other_terms = products(pl.ds(other, HALF))
    logits, gate_part, up_part = [a + b for a, b in zip(own_terms, other_terms)]
    expert = lax.broadcasted_iota(jnp.int32, (EXPERTS, TOK), 0).astype(F32)
    member = (wanted[0:1] == expert) | (wanted[1:2] == expert)
    raised = jnp.where(member, jnp.exp(logits), 0.0)
    mine = jnp.sum(jnp.where(expert == zh.astype(F32), raised, 0.0), axis=0, keepdims=True)
    gate = mine / jnp.sum(raised, axis=0, keepdims=True)
    hidden = (gate_part / (1.0 + jnp.exp(-gate_part)) * up_part * gate).T
    hb[:, 0:FFW] = hidden.astype(BF16)
    hb_copy = push(hb.at[:, 0:FPAD], hb.at[:, FPAD : 2 * FPAD], pr_ss.at[3], pr_rs.at[3], partner)
    wd_copy.wait_recv()
    hb_copy.wait_recv()
    units = hb[...]

    own_rows = lax.broadcasted_iota(jnp.int32, (CH, W), 0) // GR == zh
    for piece, value in reduce_rows(
        lambda piece: dot(units, wd2[:, cols_of(piece)]), s2, r2, s2_ss, s2_rs
    ):
        cols = cols_of(piece)
        rows = mx[
            pl.ds(pl.multiple_of(y * CH, CH), CH),
            pl.ds(pl.multiple_of(c * HALF + piece * W, W), W),
        ].astype(F32)
        value = value + jnp.where(own_rows, rows, 0.0)
        for g in range(NZH):
            for k in (0, 1):
                rows = value[g * GR + 2 * k : g * GR + 2 * k + 2, :]
                f_acc[g, k, :, cols] = rows
                f_s[g, k, :, cols] = rows.astype(BF16)

    earlier, sent[:] = list(sent), []
    for d in (2, 1, 3):
        to = (zh + d) % NZH
        for k in (0, 1):
            push(
                f_s.at[to, k], f_r.at[d - 1, c], f_ss.at[d - 1, k], f_rs.at[d - 1, c],
                (seq, exp_id(to, y, k)),
            )
    push(f_acc.at[zh, 1 - c], f_own.at[c], f_ss.at[3, 0], f_rs.at[3, 0], partner)
    f_own[c] = f_acc[zh, c]
    for copy in earlier:
        copy.wait_send()

    @pl.when(zl <= 1)
    def _():
        rows_up[0].wait_send()

    @pl.when(zl == 0)
    def _():
        rows_up[1].wait_send()

    remote(f_acc.at[zh, 1 - c], f_own.at[1 - c], f_ss.at[3, 0], f_rs.at[3, 0], partner).wait_recv()
    for d in (1, 3, 2):
        for k in (0, 1):
            remote(
                f_s.at[0, k], f_r.at[d - 1, k], f_ss.at[d - 1, k], f_rs.at[d - 1, k], partner
            ).wait_recv()
    for k in (0, 1):
        value = f_own[k]
        for d in range(3):
            value = value + f_r[d, k].astype(F32)
        out_ref[:, k * HALF : (k + 1) * HALF] = value.astype(BF16)

    for copy in sent:
        copy.wait_send()


def layer(query, key_in, value, decay_log, norm_gain, w_out, router, routes, w_gate, w_up, w_down):
    dma = pltpu.SemaphoreType.DMA
    return pl.pallas_call(
        kernel,
        out_shape=pltpu.VMEM((2, DM), BF16),
        in_specs=[pl.BlockSpec(memory_space=pl.ANY)] * 11,
        out_specs=pl.BlockSpec(memory_space=pltpu.VMEM),
        scratch_shapes=[
            pltpu.VMEM((TOK, HEAD), BF16),
            pltpu.VMEM((TOK, HEAD), BF16),
            pltpu.VMEM((TOK, HEAD), BF16),
            pltpu.VMEM((1, TOK), F32),
            pltpu.VMEM((1, HEAD), BF16),
            pltpu.VMEM((2 * HEAD, HALF), BF16),
            pltpu.VMEM((EXPERTS, DM), BF16),
            pltpu.VMEM((2, TOK), jnp.int32),
            pltpu.VMEM((FFW, DM), BF16),
            pltpu.VMEM((FFW, DM), BF16),
            pltpu.VMEM((2 * FPAD, HALF), BF16),
            pltpu.VMEM((PACK, HEAD), BF16),
            pltpu.VMEM((3, PACK, HEAD), BF16),
            pltpu.VMEM((PACK, HEAD), BF16),
            pltpu.VMEM((2, PACK, HEAD), BF16),
            pltpu.VMEM((TOK, HEAD), F32),
            pltpu.VMEM((TOK, 2 * HEAD), BF16),
            pltpu.VMEM((TOK, HALF), F32),
            pltpu.VMEM((2, 4, CH, HALF), BF16),
            pltpu.VMEM((2, 4, CH, HALF), BF16),
            pltpu.VMEM((CH, HALF), F32),
            pltpu.VMEM((2, CH, HALF), BF16),
            pltpu.VMEM((2, CH, HALF), BF16),
            pltpu.VMEM((TOK, DM), BF16),
            pltpu.VMEM((TOK, 2 * FPAD), BF16),
            pltpu.VMEM((2, 4, CH, HALF), BF16),
            pltpu.VMEM((2, 4, CH, HALF), BF16),
            pltpu.VMEM((NZH, 2, 2, HALF), F32),
            pltpu.VMEM((NZH, 2, 2, HALF), BF16),
            pltpu.VMEM((3, 2, 2, HALF), BF16),
            pltpu.VMEM((2, 2, HALF), F32),
            dma((11,)),
            dma((3,)),
            dma((3,)),
            dma((2,)),
            dma((2,)),
            dma((4,)),
            dma((4,)),
            dma((2, 4, NP)),
            dma((2, 4, NP)),
            dma((2, NP)),
            dma((2, NP)),
            dma((2, 4, NP)),
            dma((2, 4, NP)),
            dma((8,)),
            dma((8,)),
            dma((2, 4, NP)),
            dma((2, 4, NP)),
            dma((4, 2)),
            dma((4, 2)),
        ],
        compiler_params=pltpu.CompilerParams(
            collective_id=0, has_side_effects=True, vmem_limit_bytes=56 << 20
        ),
        name="layer",
    )(
        query,
        key_in,
        value,
        decay_log.T,
        norm_gain.reshape(1, HEAD),
        w_out,
        router.T,
        routes.T,
        w_gate[0].T,
        w_up[0].T,
        w_down[0],
    )


def solution(mesh):
    placed = (
        P("seq", "exp"),
        P("seq", "exp"),
        P("seq", "exp"),
        P("seq", "exp"),
        P("exp"),
        P("exp", None),
        P(),
        P("seq", None),
        P("exp", None, None),
        P("exp", None, None),
        P("exp", None, None),
    )
    return jax.shard_map(
        layer, mesh=mesh, in_specs=placed, out_specs=P(("seq", "exp"), None), check_vma=False
    )
```
